32 devices in a mesh: row: 8 (over y, x, core), col: 4 (over z).
Axes of the slice: x: 2, y: 2, z: 4, core: 2. Of those that a mesh axis runs over, the one named last changes fastest.
Arguments:
- features: bfloat16 [16384, 512], P(('row', 'col')), may hold values from -6 to 6
- weight: bfloat16 [512, 512], replicated, may hold values from -0.25 to 0.25
- bias: float32 [512], replicated, may hold values from -3 to 3
- cotangent: bfloat16 [16384, 512], P(('row', 'col')), may hold values from -6 to 6
- tile_values: bfloat16 [8, 4, 64, 128, 128], P('row', 'col'), may hold values from -0.1875 to 0.1875
- tile_rows: int32 [8, 4, 64], P('row', 'col'), may hold values from 0 to 127, as said below
- tile_cols: int32 [8, 4, 64], P('row', 'col'), may hold values from 0 to 127, as said below
- tile_counts: int32 [8, 4], P('row', 'col'), may hold values from 1 to 64
Outputs:
- output: bfloat16 [16384, 512], P(('row', 'col'))
- feature_grad: bfloat16 [16384, 512], P(('row', 'col'))
- weight_grad: float32 [512, 512], replicated
- bias_grad: float32 [512], replicated
The draws below stay inside these ranges and needn't reach their ends.
Inputs may be any that keep to these rules, and one draw needn't show every extreme that they name: `tile_rows`: A tile on device (p, q) has its row block in row group p, that is row block // 16 == p, and its column block's atoms on devices of index q along col, that is (column block // 4) % 4 == q. The rows of features held by device (p, q) are blocks p * 4 * 4 + q * 4 to that plus 4 - 1. Row and column pairs may repeat. `tile_cols`: among one device's live tiles at most 16 have their row block held by any one device of that row group, and at most 8 have their column block held by any one device of that column group.
All inputs are finite; a program needn't handle non-finite values.
Results may differ from the reference program's by a relative error of at most 0.013.
Values may be sent and summed in bfloat16 or wider, within the bound.
A program may use at most 128 MiB of HBM per device.

```python
import math
import jax
import jax.numpy as jnp
from jax import lax

D = 512
BS = 128
BLK_DEV = 4
KMAX = 64
BLOCKS = 128
ATOMS = 16384
N_ROW = 8
N_COL = 4


def slot_order(sub_key):
    return jax.random.permutation(sub_key, KMAX)


def tile_layout(key):
    base_key = jax.random.fold_in(key, 4711)
    key_list = jax.random.split(base_key, 5)
    device_total = N_ROW * N_COL
    full_device = jax.random.randint(key_list[0], (), 0, device_total)
    partial_counts = jax.random.randint(key_list[1], (device_total,), KMAX // 4, 3 * KMAX // 4 + 1)
    counts = jnp.where(jnp.arange(device_total) == full_device, KMAX, partial_counts).astype(jnp.int32)
    orders = jax.vmap(slot_order)(jax.random.split(key_list[2], device_total)).astype(jnp.int32)
    row_owner = orders % N_ROW
    col_owner = (orders // N_ROW + orders) % N_COL
    device_ids = jnp.arange(device_total, dtype=jnp.int32)
    device_rows = (device_ids // N_COL)[:, None]
    device_cols = (device_ids % N_COL)[:, None]
    row_pick = jax.random.randint(key_list[3], (device_total, KMAX), 0, BLK_DEV)
    col_pick = jax.random.randint(key_list[4], (device_total, KMAX), 0, BLK_DEV)
    rows = device_rows * (BLK_DEV * N_COL) + col_owner * BLK_DEV + row_pick
    cols = row_owner * (BLK_DEV * N_COL) + device_cols * BLK_DEV + col_pick
    return (rows.reshape(N_ROW, N_COL, KMAX).astype(jnp.int32), cols.reshape(N_ROW, N_COL, KMAX).astype(jnp.int32), counts.reshape(N_ROW, N_COL))


def draw_tile_rows(key, part):
    return tile_layout(key)[0]


def draw_tile_cols(key, part):
    return tile_layout(key)[1]


def draw_tile_counts(key, part):
    return tile_layout(key)[2]


def shard_levels(stream_key, dims, pieces, low, top_value):
    factor_of, own = 1.0, jax.random.fold_in(stream_key, 6)
    for dim, blocks in pieces:
        draws = jnp.exp(jax.random.uniform(jax.random.fold_in(own, dim), (blocks,), jnp.float32, low / len(pieces), top_value / len(pieces)))
        factor_of = factor_of * jnp.repeat(draws, dims[dim] // blocks).reshape([-1 if axis == dim else 1 for axis in range(len(dims))])
    return factor_of


def scatter_about(key, extent, scale, reach, cuts=(), kind=jnp.bfloat16):
    loudness = shard_levels(key, extent, cuts, -0.22, 0.18) if cuts else 1.0
    drawn = jax.random.normal(key, extent, jnp.float32) * scale * loudness
    return jnp.minimum(jnp.maximum(drawn, -reach), reach).astype(kind)


def setup_inputs(seed: int = 0) -> dict:
    keys = jax.random.split(jax.random.key(seed), 9)
    features = scatter_about(keys[0], (ATOMS, D), 1.0, 6.0, ((0, 32),))
    weight = scatter_about(keys[1], (D, D), D ** -0.5, 0.25)
    bias = scatter_about(keys[2], (D,), 0.5, 3.0, (), jnp.float32)
    cotangent = scatter_about(keys[3], (ATOMS, D), 1.0, 6.0, ((0, 32),))
    tile_values = scatter_about(keys[4], (N_ROW, N_COL, KMAX, BS, BS), (8 * BS) ** -0.5, 0.1875, ((0, 8), (1, 4)))
    tile_rows = draw_tile_rows(jax.random.fold_in(keys[8], 71), 0)
    tile_cols = draw_tile_cols(jax.random.fold_in(keys[8], 71), 0)
    tile_counts = draw_tile_counts(jax.random.fold_in(keys[8], 71), 0)
    return dict(features=features, weight=weight, bias=bias, cotangent=cotangent, tile_values=tile_values, tile_rows=tile_rows, tile_cols=tile_cols, tile_counts=tile_counts)


def block_products(tiles, alive, source_blocks, fetch_ids, add_ids, transpose):

    def step(carry, items):
        tile_group, fetch_row, add_row, alive_row = items
        picked = source_blocks[fetch_row].astype(jnp.float32)
        mats = tile_group.astype(jnp.float32)
        if transpose:
            products = jnp.einsum('kba,kbd->kad', mats, picked)
        else:
            products = jnp.einsum('kab,kbd->kad', mats, picked)
        products = products * alive_row.astype(jnp.float32)[:, None, None]
        return (carry.at[add_row].add(products), None)
    initial = jnp.zeros((BLOCKS, BS, D), jnp.float32)
    total, unused = lax.scan(step, initial, (tiles, fetch_ids, add_ids, alive))
    return total.reshape(ATOMS, D)

def reference(features, weight, bias, cotangent, tile_values, tile_rows, tile_cols, tile_counts):
    device_total = N_ROW * N_COL
    tiles = tile_values.reshape(device_total, KMAX, BS, BS)
    row_ids = tile_rows.reshape(device_total, KMAX).astype(jnp.int32)
    col_ids = tile_cols.reshape(device_total, KMAX).astype(jnp.int32)
    alive = jnp.arange(KMAX, dtype=jnp.int32)[None, :] < tile_counts.reshape(device_total, 1)
    feature_blocks = features.reshape(BLOCKS, BS, D)
    aggregated = block_products(tiles, alive, feature_blocks, col_ids, row_ids, False).astype(jnp.bfloat16)
    pre_act = jnp.dot(aggregated, weight, preferred_element_type=jnp.float32) + bias.astype(jnp.float32)
    sigm = jax.nn.sigmoid(pre_act)
    output = (pre_act * sigm).astype(jnp.bfloat16)
    grad_pre = (cotangent.astype(jnp.float32) * sigm * (1.0 + pre_act * (1.0 - sigm))).astype(jnp.bfloat16)
    scale = 1.0 / math.sqrt(ATOMS)
    weight_grad = jnp.dot(aggregated.T, grad_pre, preferred_element_type=jnp.float32) * scale
    bias_grad = lax.optimization_barrier(jnp.sum(grad_pre.astype(jnp.float32), axis=0)) * scale
    grad_agg = jnp.dot(grad_pre, weight.T, preferred_element_type=jnp.float32).astype(jnp.bfloat16)
    grad_blocks = grad_agg.reshape(BLOCKS, BS, D)
    feature_grad = block_products(tiles, alive, grad_blocks, row_ids, col_ids, True).astype(jnp.bfloat16)
    return (output, feature_grad, weight_grad, bias_grad)
```

```python
import functools
import math
import types

import jax
import jax.numpy as jnp
from jax import lax
from jax.experimental import pallas as pl
from jax.experimental.pallas import tpu as pltpu
from jax.sharding import PartitionSpec as P

MESH = pl.DeviceIdType.MESH
BF = jnp.bfloat16
F32 = jnp.float32
PAD = 16
LANE = 128
LISTS = 6


def flip(k, d):
    out = 0
    for b in range(8):
        step = 1 << b
        if isinstance(d, int):
            if d < step:
                bit = 0
            else:
                bit = (d // step) % 2
        else:
            bit = (d // step) % 2
        kb = (k // step) % 2
        if isinstance(bit, int):
            out = out + step * ((1 - kb) if bit else kb)
        else:
            out = out + step * (kb + bit - 2 * kb * bit)
    return out


def remote(src, dst, send, recv, to):
    return pltpu.make_async_remote_copy(
        src_ref=src, dst_ref=dst, send_sem=send, recv_sem=recv, device_id=to, device_id_type=MESH
    )


def list_kernel(nrow, ncol, blk, counts, rows, cols, out, lens):
    slots = rows.shape[0]
    capf, capb = slots // ncol, slots // nrow
    span = blk * ncol

    @pl.loop(0, slots)
    def _(i):
        out[i] = 0
        out[slots + i] = -1
        out[2 * slots + i] = 0
        out[3 * slots + i] = 0
        out[4 * slots + i] = -1
        out[5 * slots + i] = 0

    @pl.loop(0, nrow + ncol)
    def _(i):
        lens[i] = 0

    @pl.loop(0, counts[0])
    def _(k):
        row = rows[k] % span
        col = cols[k]
        o = row // blk
        at = o * capf + lens[o]
        lens[o] = lens[o] + 1
        dev = col // span
        src = dev * blk + col % blk
        out[at] = k
        out[slots + at] = row % blk
        out[2 * slots + at] = src
        bt = dev * capb + lens[ncol + dev]
        lens[ncol + dev] = lens[ncol + dev] + 1
        out[3 * slots + bt] = k
        out[4 * slots + bt] = col % blk
        out[5 * slots + bt] = row


def add_rows(dst, srcs, begin, count):
    step = 64

    @pl.loop(0, count // step)
    def _(i):
        at = pl.ds(pl.multiple_of(begin + i * step, step), step)
        total = srcs[0][at, :].astype(F32)
        for s in srcs[1:]:
            total = total + s[at, :].astype(F32)
        dst[at, :] = total.astype(dst.dtype)


def weight_block(parts, scale, agg, gp, wp):
    width = agg.shape[1]
    rows = width // (2 * parts)
    total = jnp.sum(gp[...].astype(F32), axis=0, keepdims=True) * scale
    pad = jnp.broadcast_to(total, (PAD, width)).astype(BF)
    step = 128
    for t in range(width // step):
        res = lax.dot_general(
            agg[:, t * step : (t + 1) * step],
            gp[...],
            (((0,), (0,)), ((), ())),
            preferred_element_type=F32,
        )
        res = (res * scale).astype(BF)
        for u in range(step // rows):
            p = (t * step) // rows + u
            wp[p // parts, p % parts, :rows, :] = res[u * rows : (u + 1) * rows]
            wp[p // parts, p % parts, rows:, :] = pad


def mega_kernel(
    names, n, nrow, nb, scale, wb, lists, feats, tiles_in, w, bias, cot, out, fg, w4, bg, *scratch
):
    v = types.SimpleNamespace(**dict(zip(names, scratch)))
    r, q = lax.axis_index("row"), lax.axis_index("col")
    k, c = r // 2, r % 2
    chips = nrow // 2
    last = n - 1
    right, left = (r, jnp.minimum(q + 1, last)), (r, jnp.maximum(q - 1, 0))
    partner = (k * 2 + 1 - c, q)
    relay = chips == 4
    near = [d for d in range(1, chips) if not (relay and d == 3)]
    hb = nb // 2
    slots, size = v.tiles.shape[0], v.tiles.shape[1]
    rows = nb * size
    capf, capb = slots // n, slots // nrow
    kparts = capf // capb
    width = w.shape[0]
    nch = width // LANE
    npa = v.pa.shape[0] // n
    arows = rows // npa
    npb = v.pb.shape[0] // n
    piece = rows // npb
    ppb = size // piece
    xg = [getattr(v, "x%d" % j) for j in range(nch)]
    sp = [v.sp0, v.sp1]
    grads = [v.g0, v.g1]
    abuf, bbuf, cbuf = [v.a0, v.a1], [v.b0, v.b1], [v.c0, v.c1]

    def dev(d):
        return (flip(k, d) * 2 + c, q)

    def deep(dz):
        return (r, (q + dz) % n)


    def take(j):
        return pltpu.make_async_copy(
            feats.at[:, :, pl.ds(j * LANE, LANE)], xg[j].at[pl.ds(r * nb, nb)], v.s_take.at[j]
        )

    def slot(j, d, core, h):
        return xg[j].at[pl.ds((flip(k, d) * 2 + core) * nb + h * hb, hb)]

    def own(j, d, h):
        return remote(
            slot(j, 0, c, h), slot(j, 0, c, h), v.s_same.at[j, d, h], v.r_same.at[j, d, h], dev(d)
        )

    def pass_on(j, h):
        via, to = (1, 2) if h == 0 else (2, 1)
        return remote(
            slot(j, via, c, h), slot(j, via, c, h), v.s_same.at[j, 3, h], v.r_same.at[j, 3, h], dev(to)
        )

    def inc(j, d, h):
        return remote(
            slot(j, d, c, h), slot(j, d, c, h), v.s_same.at[j, d, h], v.r_same.at[j, d, h], dev(d)
        )

    def fwd(j, d, h):
        return remote(
            slot(j, d, c, h), slot(j, d, c, h), v.s_part.at[j, d, h], v.r_part.at[j, d, h], partner
        )

    def inc_part(j, d, h):
        return remote(
            slot(j, d, 1 - c, h),
            slot(j, d, 1 - c, h),
            v.s_part.at[j, d, h],
            v.r_part.at[j, d, h],
            partner,
        )

    def gather_start(j):
        take(j).wait()
        for i in range(2):
            for d in near:
                own(j, d, (i + (d == 2)) % 2).start()
        for h in range(2):
            fwd(j, 0, h).start()

    def gather_mid(j):
        for i in range(2):
            for d in near:
                h = (i + (d == 2)) % 2
                inc(j, d, h).wait_recv()
                if relay and i == 0:
                    pass_on(j, h).start()
                fwd(j, d, h).start()

    def gather_end(j):
        if relay:
            for h in range(2):
                inc(j, 3, h).wait_recv()
                fwd(j, 3, h).start()
        for d in range(chips):
            for h in range(2):
                inc_part(j, d, h).wait_recv()

    def gather_sent(j):
        for h in range(2):
            for d in near:
                own(j, d, h).wait_send()
            if relay:
                pass_on(j, h).wait_send()
            for d in range(chips):
                fwd(j, d, h).wait_send()


    def build(o, base, cap, back):
        for s in range(cap):
            at = o * cap + s
            mat = v.tiles[lists[base * slots + at]]
            place = lists[(base + 1) * slots + at]
            if back:
                mat = jnp.transpose(mat)
            for b in range(nb):
                val = jnp.where(place == b, mat, jnp.zeros_like(mat))
                if back:
                    v.dense[o, b * size : (b + 1) * size, s * size : (s + 1) * size] = val
                else:
                    u = s % capb
                    v.dense[
                        o * kparts + s // capb, b * size : (b + 1) * size, u * size : (u + 1) * size
                    ] = val

    def forward(j):
        @pl.loop(0, n)
        def _(o):
            total = None
            for e in range(kparts):
                ids = [lists[2 * slots + o * capf + e * capb + s] for s in range(capb)]
                rhs = jnp.concatenate([xg[j][i] for i in ids], axis=0)
                res = jnp.dot(v.dense[o * kparts + e], rhs, preferred_element_type=F32)
                total = res if total is None else total + res
            total = total.astype(BF)
            if j == 0:
                v.pa[pl.ds(o * npa, npa)] = total.reshape(npa, arows, LANE)
            else:
                v.pb[pl.ds(o * npb, npb), :, (j - 1) * LANE : j * LANE] = total.reshape(
                    npb, piece, LANE
                )

    def backward(g, o):
        ids = [lists[5 * slots + o * capb + s] for s in range(capb)]
        rhs = jnp.concatenate([sp[g][i] for i in ids], axis=0)
        grads[g][o] = jnp.dot(v.dense[o], rhs, preferred_element_type=F32).astype(BF)


    def chain(part, acc, count, sems, names_at, to, shift, d, j, first):
        at = (d + shift) * count + j
        src = part.at[d * count + j] if first else acc.at[at]
        return remote(src, acc.at[at], sems[names_at].at[d, j], sems[names_at + 1].at[d, j], to)

    def group(part, acc, count, sems):
        def cp_r(d, j, first=False):
            return chain(part, acc, count, sems, 0, right, 1, d, j, first)

        def cp_l(d, j, first=False):
            return chain(part, acc, count, sems, 2, left, 0, d, j, first)

        def hop(cp, shift, start, d, j):
            @pl.when(start)
            def _():
                cp(d, j, True).start()

            @pl.when(jnp.logical_not(start))
            def _():
                cp(d, j).wait_recv()
                at = (d + shift) * count + j
                acc[at] = (acc[at].astype(F32) + part[d * count + j].astype(F32)).astype(BF)
                cp(d, j).start()

        def live(j):
            return jnp.logical_and(j >= 0, j < count)

        def reduce_step(t):
            jr, jl = t - q, t - (last - q)

            @pl.when(live(jr))
            def _():
                @pl.loop(0, last - q)
                def _(i):
                    hop(cp_r, 1, q == 0, last - i, jr)

            @pl.when(live(jl))
            def _():
                @pl.loop(0, q)
                def _(i):
                    hop(cp_l, 0, q == last, i, jl)

        def total(j, buf):
            buf[...] = part[q * count + j].astype(F32)

            @pl.when(q > 0)
            def _():
                cp_r(q, j).wait_recv()
                buf[...] += acc[(q + 1) * count + j].astype(F32)

            @pl.when(q < last)
            def _():
                cp_l(q, j).wait_recv()
                buf[...] += acc[q * count + j].astype(F32)

        def sent():
            @pl.loop(0, count)
            def _(j):
                for d in range(n):
                    @pl.when(q < d)
                    def _():
                        cp_r(d, j).wait_send()

                    @pl.when(q > d)
                    def _():
                        cp_l(d, j).wait_send()

        return types.SimpleNamespace(live=live, reduce_step=reduce_step, total=total, sent=sent)

    ga = group(v.pa, v.acca, npa, [v.sa_r, v.ra_r, v.sa_l, v.ra_l])
    gb = group(v.pb, v.accb, npb, [v.sb_r, v.rb_r, v.sb_l, v.rb_l])


    def part_of(d, j):
        at = d * npb + j
        return at // ppb, pl.ds(pl.multiple_of((at % ppb) * piece, piece), piece)

    def cp_g(s, rs, to, d, j):
        b, at = part_of(d, j)
        return remote(sp[0].at[b, at], sp[0].at[b, at], s.at[d, j], rs.at[d, j], to)

    cp_gr = functools.partial(cp_g, v.s_gr, v.r_gr, right)
    cp_gl = functools.partial(cp_g, v.s_gl, v.r_gl, left)

    def cp_h(s, rs, to, d, h):
        at = pl.ds(d * nb + h * hb, hb)
        return remote(sp[1].at[at], sp[1].at[at], s.at[d, h], rs.at[d, h], to)

    cp_hr = functools.partial(cp_h, v.s_hr, v.r_hr, right)
    cp_hl = functools.partial(cp_h, v.s_hl, v.r_hl, left)

    def send_both(cr, cl, d, j):
        @pl.when(q < last)
        def _():
            cr(d, j).start()

        @pl.when(q > 0)
        def _():
            cl(d, j).start()

    def relay_on(cr, cl, ok, j, o):
        @pl.when(jnp.logical_and(ok, q >= o))
        def _():
            cr(q - o, j).wait_recv()

            @pl.when(q < last)
            def _():
                cr(q - o, j).start()

        @pl.when(jnp.logical_and(ok, q + o <= last))
        def _():
            cl(q + o, j).wait_recv()

            @pl.when(q > 0)
            def _():
                cl(q + o, j).start()

    def relay_rest(o):
        for h in range(2):
            relay_on(cp_hr, cp_hl, True, h, o)

    def sent_on(cr, cl, count):
        @pl.loop(0, count)
        def _(j):
            for d in range(n):
                @pl.when(jnp.logical_and(q >= d, q < last))
                def _():
                    cr(d, j).wait_send()

                @pl.when(jnp.logical_and(q <= d, q > 0))
                def _():
                    cl(d, j).wait_send()

    def finish_a(j):
        ga.total(j, v.fa)
        v.agg[pl.ds(pl.multiple_of(j * arows, arows), arows), :LANE] = v.fa[...].astype(BF)

    def finish(j):
        gb.total(j, v.fb)
        at = pl.ds(pl.multiple_of(j * piece, piece), piece)
        v.agg[at, LANE:] = v.fb[...].astype(BF)
        pre = jnp.dot(v.agg[at, :], w[...], preferred_element_type=F32) + bias[...]
        sig = jax.nn.sigmoid(pre)
        out[at, :] = (pre * sig).astype(BF)
        g = (cot[at, :].astype(F32) * sig * (1.0 + pre * (1.0 - sig))).astype(BF)
        v.gp[at, :] = g
        res = lax.dot_general(
            g, w[...], (((1,), (1,)), ((), ())), preferred_element_type=F32
        ).astype(BF)
        b, sub = part_of(q, j)
        sp[0][b, sub, :] = res[:, : wb[0]]
        sp[1][b, sub, :] = res[:, wb[0] :]
        send_both(cp_gr, cp_gl, q, j)


    cp_w1 = remote(v.wp.at[1 - c], v.w1, v.s_w1.at[0], v.r_w1.at[0], partner)

    def cp_w2(d):
        return remote(v.w1.at[flip(k, d)], v.w2.at[d], v.s_w2.at[d], v.r_w2.at[d], dev(d))

    def cp_w3(dz):
        return remote(v.ws, v.w3.at[q], v.s_w3.at[dz], v.r_w3.at[dz], deep(dz))

    def cp_w4(d):
        return remote(w4.at[c, k], w4.at[c, k], v.s_w4.at[d], v.r_w4.at[d], dev(d))

    def cp_w5(d):
        at = flip(k, d)
        return remote(w4.at[c, at], w4.at[c, at], v.s_w5.at[d], v.r_w5.at[d], partner)

    def weight_1():
        cp_w1.wait_recv()
        for z in range(chips):
            v.w1[z] = (v.w1[z].astype(F32) + v.wp[c, z].astype(F32)).astype(BF)
        for d in range(1, chips):
            cp_w2(d).start()

    def weight_2():
        total = v.w1[k].astype(F32)
        for d in range(1, chips):
            cp_w2(d).wait_recv()
            total = total + v.w2[d].astype(F32)
        v.ws[...] = total.astype(BF)
        for dz in range(1, n):
            cp_w3(dz).start()

    def weight_3():
        v.w3[q] = v.ws[...]
        for dz in range(1, n):
            at = (q + n - dz) % n
            remote(v.w3.at[at], v.w3.at[at], v.s_w3.at[dz], v.r_w3.at[dz], deep(dz)).wait_recv()
        total = v.w3[0].astype(F32)
        for i in range(1, n):
            total = total + v.w3[i].astype(F32)
        w4[c, k] = total.astype(BF)
        for d in range(1, chips):
            cp_w4(d).start()
        cp_w5(0).start()

    def weight_4():
        for d in range(1, chips):
            at = flip(k, d)
            remote(w4.at[c, at], w4.at[c, at], v.s_w4.at[d], v.r_w4.at[d], dev(d)).wait_recv()
            cp_w5(d).start()

    def weight_5():
        for d in range(chips):
            at = flip(k, d)
            remote(
                w4.at[1 - c, at], w4.at[1 - c, at], v.s_w5.at[d], v.r_w5.at[d], partner
            ).wait_recv()
        bg[...] = w4[0, 0, w4.shape[2] - PAD :, :].astype(F32)[:1]

    def weight_sent():
        cp_w1.wait_send()
        for d in range(1, chips):
            cp_w2(d).wait_send()
            cp_w4(d).wait_send()
        for dz in range(1, n):
            cp_w3(dz).wait_send()
        for d in range(chips):
            cp_w5(d).wait_send()


    half = rows // 2

    def mine(g, d):
        return grads[g].at[flip(k, d) * 2 + c]

    def cp_a(g, d):
        return remote(
            grads[g].at[flip(k, d) * 2 + 1 - c],
            abuf[g].at[d],
            v.s_a.at[g, d],
            v.r_a.at[g, d],
            partner,
        )

    def cp_b(g, d, h):
        at = pl.ds(h * half, half)
        return remote(
            abuf[g].at[d, at], bbuf[g].at[d, at], v.s_b.at[g, d, h], v.r_b.at[g, d, h], dev(d)
        )

    def cp_c(g, h):
        return remote(
            abuf[g].at[3, pl.ds(h * half, half)],
            cbuf[g].at[h],
            v.s_c.at[g, h],
            v.r_c.at[g, h],
            dev(h + 1),
        )

    def join(g, d):
        cp_a(g, d).wait_recv()
        add_rows(abuf[g].at[d], [abuf[g].at[d], mine(g, d)], 0, rows)

    def products(g, lo, hi):
        @pl.loop(lo, hi)
        def _(i):
            d = chips - 1 - i
            at = flip(k, d) * 2
            backward(g, at + 1 - c)
            cp_a(g, d).start()
            backward(g, at + c)

    def rows_1(g):
        if relay:
            join(g, 3)
            cp_c(g, 0).start()
            cp_c(g, 1).start()
            join(g, 2)
            cp_b(g, 2, 1).start()
            join(g, 1)
            cp_b(g, 1, 0).start()
        else:
            for d in range(chips - 1, 0, -1):
                join(g, d)
                for h in range(2):
                    cp_b(g, d, h).start()

    def rows_2(g):
        if relay:
            cp_c(g, 0).wait_recv()
            add_rows(abuf[g].at[2], [abuf[g].at[2], cbuf[g].at[0]], 0, half)
            cp_b(g, 2, 0).start()
            cp_c(g, 1).wait_recv()
            at = pl.ds(half, half)
            add_rows(abuf[g].at[1, at], [abuf[g].at[1, at], cbuf[g].at[1]], 0, half)
            cp_b(g, 1, 1).start()
        join(g, 0)

    def rows_3(g):
        for h in range(2):
            for d in near:
                cp_b(g, d, (h + (d == 2)) % 2).wait_recv()
        begin = 0 if g == 0 else wb[0]
        dst = fg.at[:, pl.ds(begin, wb[g])]
        add_rows(dst, [abuf[g].at[0]] + [bbuf[g].at[d] for d in near], 0, rows)

    def rows_sent(g):
        for d in range(chips):
            cp_a(g, d).wait_send()
        for d in near:
            for h in range(2):
                cp_b(g, d, h).wait_send()
        if relay:
            for h in range(2):
                cp_c(g, h).wait_send()


    barrier = pltpu.get_barrier_semaphore()
    peers = [partner] + [dev(d) for d in range(1, chips)] + [deep(dz) for dz in range(1, n)]
    for peer in peers:
        pl.semaphore_signal(barrier, inc=1, device_id=peer, device_id_type=MESH)
    load = pltpu.make_async_copy(tiles_in, v.tiles, v.s_load.at[0])
    for j in range(nch):
        take(j).start()
    load.start()
    pl.semaphore_wait(barrier, len(peers))

    gather_start(0)
    gather_start(1)
    load.wait()

    @pl.loop(0, n)
    def _(o):
        build(o, 0, capf, False)

    for j in range(nch):
        gather_mid(j)
        if j + 2 < nch:
            gather_start(j + 2)
        gather_end(j)
        forward(j)
        if j < npa:
            ga.reduce_step(j)

    done = npa + npb + last - 1

    @pl.loop(min(nch, npa), npa + npb + 2 * last)
    def _(t):
        ga.reduce_step(t)
        gb.reduce_step(t - npa)
        for o in range(1, n):
            j = t - npa - last - o
            relay_on(cp_gr, cp_gl, gb.live(j), j, o)

        for e in range(npa):
            @pl.when(t == max(nch, npa, last + e))
            def _():
                finish_a(e)

        j = t - npa - last

        @pl.when(gb.live(j))
        def _():
            finish(j)

        o = t - npa

        @pl.when(jnp.logical_and(o >= 0, o < nrow))
        def _():
            build(o, 3, capb, True)

        @pl.when(t == done)
        def _():
            for h in range(2):
                send_both(cp_hr, cp_hl, q, h)
            weight_block(chips, scale, v.agg, v.gp, v.wp)
            cp_w1.start()

        @pl.when(t == done + 1)
        def _():
            weight_1()

    mid = chips // 2
    relay_rest(1)
    products(0, 0, mid)
    weight_2()
    for o in range(2, n - 1):
        relay_rest(o)
    products(0, mid, chips)
    rows_1(0)
    for o in range(max(2, n - 1), n):
        relay_rest(o)
    weight_3()
    products(1, 0, chips)
    rows_2(0)
    rows_1(1)
    weight_4()
    rows_3(0)
    rows_2(1)
    weight_5()
    rows_3(1)

    for j in range(nch):
        gather_sent(j)
    ga.sent()
    gb.sent()
    sent_on(cp_gr, cp_gl, npb)
    sent_on(cp_hr, cp_hl, 2)
    rows_sent(0)
    rows_sent(1)
    weight_sent()


def tail_kernel(out_in, fg_in, parts, bg_in, out, fg, wg, bg, sems):
    one = pltpu.make_async_copy(out_in, out, sems.at[0])
    two = pltpu.make_async_copy(fg_in, fg, sems.at[1])
    one.start()
    two.start()
    chips = parts.shape[1]
    rows = wg.shape[0] // (2 * chips)
    for a in range(2):
        for b in range(chips):
            at = (a * chips + b) * rows
            wg[at : at + rows, :] = parts[a, b, :rows, :].astype(F32)
    bg[...] = bg_in[...]
    one.wait()
    two.wait()


VM = pl.BlockSpec(memory_space=pltpu.VMEM)
SM = pl.BlockSpec(memory_space=pltpu.SMEM)
ANY = pl.BlockSpec(memory_space=pl.ANY)


def dma(*shape):
    return pltpu.SemaphoreType.DMA(shape)


def on_device(features, weight, bias, cotangent, tile_values, tile_rows, tile_cols, tile_counts):
    nrow = lax.axis_size("row")
    ncol = lax.axis_size("col")
    node_dev, width = features.shape
    slots, size = tile_values.shape[2], tile_values.shape[3]
    nb = node_dev // size
    chips = nrow // 2
    scale = 1.0 / math.sqrt(node_dev * nrow * ncol)
    values = tile_values.reshape(slots, size, size)

    lists = pl.pallas_call(
        functools.partial(list_kernel, nrow, ncol, nb),
        out_shape=jax.ShapeDtypeStruct((LISTS * slots,), jnp.int32),
        in_specs=[SM, SM, SM],
        out_specs=SM,
        scratch_shapes=[pltpu.SMEM((nrow + ncol,), jnp.int32)],
        name="lists",
    )(tile_counts.reshape(1), tile_rows.reshape(slots), tile_cols.reshape(slots))

    nch = width // LANE
    npa = 4
    arows = node_dev // npa
    piece = size // 2
    npb = node_dev // piece
    wide = width - LANE
    wb = (width // 2, width - width // 2)
    pr = width // (2 * chips) + PAD
    capb = slots // nrow

    def vm(*shape, dtype=BF):
        return pltpu.VMEM(shape, dtype)

    scratch = {"x%d" % j: vm(nrow * nb, size, LANE) for j in range(nch)}
    scratch.update(
        tiles=vm(slots, size, size),
        dense=vm(nrow, node_dev, capb * size),
        pa=vm(ncol * npa, arows, LANE),
        pb=vm(ncol * npb, piece, wide),
        acca=vm((ncol + 1) * npa, arows, LANE),
        accb=vm((ncol + 1) * npb, piece, wide),
        fa=vm(arows, LANE, dtype=F32),
        fb=vm(piece, wide, dtype=F32),
        agg=vm(node_dev, width),
        gp=vm(node_dev, width),
        wp=vm(2, chips, pr, width),
        w1=vm(chips, pr, width),
        w2=vm(chips, pr, width),
        w3=vm(ncol, pr, width),
        ws=vm(pr, width),
        s_take=dma(nch),
        s_load=dma(1),
        s_same=dma(nch, chips, 2),
        r_same=dma(nch, chips, 2),
        s_part=dma(nch, chips, 2),
        r_part=dma(nch, chips, 2),
    )
    for g in range(2):
        scratch["sp%d" % g] = vm(ncol * nb, size, wb[g])
        scratch["g%d" % g] = vm(nrow, node_dev, wb[g])
        scratch["a%d" % g] = vm(chips, node_dev, wb[g])
        scratch["b%d" % g] = vm(chips, node_dev, wb[g])
        scratch["c%d" % g] = vm(2, node_dev // 2, wb[g])
    for name in ("sa_r", "ra_r", "sa_l", "ra_l"):
        scratch[name] = dma(ncol, npa)
    for name in ("sb_r", "rb_r", "sb_l", "rb_l", "s_gr", "r_gr", "s_gl", "r_gl"):
        scratch[name] = dma(ncol, npb)
    for name in ("s_hr", "r_hr", "s_hl", "r_hl"):
        scratch[name] = dma(ncol, 2)
    for name in ("s_a", "r_a"):
        scratch[name] = dma(2, chips)
    for name in ("s_b", "r_b"):
        scratch[name] = dma(2, chips, 2)
    for name in ("s_c", "r_c"):
        scratch[name] = dma(2, 2)
    for name in ("s_w1", "r_w1"):
        scratch[name] = dma(1)
    for name in ("s_w2", "r_w2", "s_w4", "r_w4", "s_w5", "r_w5"):
        scratch[name] = dma(chips)
    for name in ("s_w3", "r_w3"):
        scratch[name] = dma(ncol)

    out, fg, parts, bg = pl.pallas_call(
        functools.partial(mega_kernel, tuple(scratch), ncol, nrow, nb, scale, wb),
        out_shape=[
            jax.ShapeDtypeStruct((node_dev, width), BF),
            jax.ShapeDtypeStruct((node_dev, width), BF),
            jax.ShapeDtypeStruct((2, chips, pr, width), BF),
            jax.ShapeDtypeStruct((1, width), F32),
        ],
        in_specs=[SM, ANY, ANY, VM, VM, VM],
        out_specs=[VM] * 4,
        scratch_shapes=list(scratch.values()),
        compiler_params=pltpu.CompilerParams(
            collective_id=0, has_side_effects=True, vmem_limit_bytes=60 << 20
        ),
        name="layer",
    )(
        lists,
        features.reshape(nb, size, width),
        values,
        weight,
        bias.reshape(1, width),
        cotangent,
    )

    out, fg, wg, bg = pl.pallas_call(
        tail_kernel,
        out_shape=[
            jax.ShapeDtypeStruct((node_dev, width), BF),
            jax.ShapeDtypeStruct((node_dev, width), BF),
            jax.ShapeDtypeStruct((width, width), F32),
            jax.ShapeDtypeStruct((1, width), F32),
        ],
        in_specs=[ANY, ANY, VM, VM],
        out_specs=[ANY, ANY, VM, VM],
        scratch_shapes=[dma(2)],
        name="tail",
    )(out, fg, parts, bg)
    return (out, fg, wg, bg.reshape(width))


def solution(mesh):
    return jax.shard_map(
        on_device,
        mesh=mesh,
        in_specs=(
            P(("row", "col"), None),
            P(),
            P(),
            P(("row", "col"), None),
            P("row", "col", None, None, None),
            P("row", "col", None),
            P("row", "col", None),
            P("row", "col"),
        ),
        out_specs=(P(("row", "col"), None), P(("row", "col"), None), P(), P()),
        check_vma=False,
    )
```

```python
import functools
import math
import types

import jax
import jax.numpy as jnp
from jax import lax
from jax.experimental import pallas as pl
from jax.experimental.pallas import tpu as pltpu
from jax.sharding import PartitionSpec as P

MESH = pl.DeviceIdType.MESH
BF = jnp.bfloat16
F32 = jnp.float32
PAD = 16
HOP = 1
RING = 1
LISTS = 6


def flip(k, d):
    out = 0
    for b in range(8):
        step = 1 << b
        if isinstance(d, int):
            if d < step:
                bit = 0
            else:
                bit = (d // step) % 2
        else:
            bit = (d // step) % 2
        kb = (k // step) % 2
        if isinstance(bit, int):
            out = out + step * ((1 - kb) if bit else kb)
        else:
            out = out + step * (kb + bit - 2 * kb * bit)
    return out


def remote(src, dst, send, recv, to):
    return pltpu.make_async_remote_copy(
        src_ref=src, dst_ref=dst, send_sem=send, recv_sem=recv, device_id=to, device_id_type=MESH
    )


def list_kernel(nrow, ncol, blk, counts, rows, cols, out, lens):
    slots = rows.shape[0]
    capf, capb = slots // ncol, slots // nrow
    span = blk * ncol

    @pl.loop(0, slots)
    def _(i):
        out[i] = 0
        out[slots + i] = -1
        out[2 * slots + i] = 0
        out[3 * slots + i] = 0
        out[4 * slots + i] = -1
        out[5 * slots + i] = 0

    @pl.loop(0, nrow + ncol)
    def _(i):
        lens[i] = 0

    @pl.loop(0, counts[0])
    def _(k):
        row = rows[k] % span
        col = cols[k]
        o = row // blk
        at = o * capf + lens[o]
        lens[o] = lens[o] + 1
        dev = col // span
        src = dev * blk + col % blk
        out[at] = k
        out[slots + at] = row % blk
        out[2 * slots + at] = src
        bt = dev * capb + lens[ncol + dev]
        lens[ncol + dev] = lens[ncol + dev] + 1
        out[3 * slots + bt] = k
        out[4 * slots + bt] = col % blk
        out[5 * slots + bt] = row


def add_rows(dst, srcs, begin, count):
    step = 64

    @pl.loop(0, count // step)
    def _(i):
        at = pl.ds(pl.multiple_of(begin + i * step, step), step)
        total = srcs[0][at, :].astype(F32)
        for s in srcs[1:]:
            total = total + s[at, :].astype(F32)
        dst[at, :] = total.astype(dst.dtype)


def weight_block(parts, scale, agg, gp, wp):
    width = agg.shape[1]
    rows = width // (2 * parts)
    total = jnp.sum(gp[...].astype(F32), axis=0, keepdims=True) * scale
    pad = jnp.broadcast_to(total, (PAD, width)).astype(BF)
    step = 128
    for t in range(width // step):
        res = lax.dot_general(
            agg[:, t * step : (t + 1) * step],
            gp[...],
            (((0,), (0,)), ((), ())),
            preferred_element_type=F32,
        )
        res = (res * scale).astype(BF)
        for u in range(step // rows):
            p = (t * step) // rows + u
            wp[p // parts, p % parts, :rows, :] = res[u * rows : (u + 1) * rows]
            wp[p // parts, p % parts, rows:, :] = pad


def mega_kernel(
    names, n, nrow, nb, scale, wf, wb, lists, feats, tiles_in, w_in, bias, cot_in, out, fg, wg, bg,
    *scratch
):
    v = types.SimpleNamespace(**dict(zip(names, scratch)))
    r, q = lax.axis_index("row"), lax.axis_index("col")
    k, c = r // 2, r % 2
    chips = nrow // 2
    last = n - 1
    right, left = (r, jnp.minimum(q + 1, last)), (r, jnp.maximum(q - 1, 0))
    partner = (k * 2 + 1 - c, q)
    relay = chips == 4
    near = [d for d in range(1, chips) if not (relay and d == 3)]
    hb = nb // 2
    slots, size = v.tiles.shape[0], v.tiles.shape[1]
    rows = nb * size
    capf, capb = slots // n, slots // nrow
    kparts = capf // capb
    nch, ng = len(wf), len(wb)
    w, cot = v.w, v.cot
    npa = v.pa.shape[0] // n
    arows = rows // npa
    npb = v.pb.shape[0] // n
    piece = rows // npb
    ppb = size // piece
    xg = [getattr(v, "x%d" % j) for j in range(nch)]
    sp, grads, abuf, bbuf, cbuf, fgs = (
        [getattr(v, "%s%d" % (name, g)) for g in range(ng)]
        for name in ("sp", "g", "a", "b", "c", "f")
    )

    def dev(d):
        return (flip(k, d) * 2 + c, q)

    def deep(dz):
        return (r, (q + dz) % n)


    def take(j):
        return pltpu.make_async_copy(
            feats.at[:, :, pl.ds(sum(wf[:j]), wf[j])], xg[j].at[pl.ds(r * nb, nb)], v.s_take.at[j]
        )

    def slot(j, d, core, h):
        return xg[j].at[pl.ds((flip(k, d) * 2 + core) * nb + h * hb, hb)]

    def same(j, d, h, to, at):
        ref = slot(j, d, c, h)
        return remote(ref, ref, v.s_same.at[j], v.r_same.at[j, at, h], dev(to))

    def own(j, d, h):
        return same(j, 0, h, d, d)

    def pass_on(j, h):
        via, to = (1, 2) if h == 0 else (2, 1)
        return same(j, via, h, to, 3)

    def inc(j, d, h):
        return same(j, d, h, d, d)

    def fwd(j, d, h):
        ref = slot(j, d, c, h)
        return remote(ref, ref, v.s_part.at[j], v.r_part.at[j], partner)

    def gather_start(j):
        take(j).wait()
        for i in range(2):
            for d in near:
                own(j, d, (i + (d == 2)) % 2).start()
        for h in range(2):
            fwd(j, 0, h).start()

    def gather_mid(j):
        for i in range(2):
            for d in near:
                h = (i + (d == 2)) % 2
                inc(j, d, h).wait_recv()
                if relay and i == 0:
                    pass_on(j, h).start()
                fwd(j, d, h).start()

    def whole(j, count):
        ref = xg[j].at[pl.ds(0, count * nb)]
        return remote(ref, ref, v.s_part.at[j], v.r_part.at[j], partner)

    def gather_end(j):
        if relay:
            for h in range(2):
                inc(j, 3, h).wait_recv()
                fwd(j, 3, h).start()
        whole(j, chips).wait_recv()

    def gather_sent(j):
        ref = xg[j].at[pl.ds(0, (chips - 1) * nb)]
        remote(ref, ref, v.s_same.at[j], v.r_same.at[j, 0, 0], partner).wait_send()
        whole(j, chips).wait_send()


    def build(o, base, cap, back):
        for s in range(cap):
            at = o * cap + s
            mat = v.tiles[lists[base * slots + at]]
            place = lists[(base + 1) * slots + at]
            if back:
                mat = jnp.transpose(mat)
            for b in range(nb):
                val = jnp.where(place == b, mat, jnp.zeros_like(mat))
                if back:
                    v.dense[o, b * size : (b + 1) * size, s * size : (s + 1) * size] = val
                else:
                    u = s % capb
                    v.dense[
                        o * kparts + s // capb, b * size : (b + 1) * size, u * size : (u + 1) * size
                    ] = val

    def forward(j):
        @pl.loop(0, n)
        def _(o):
            total = None
            for e in range(kparts):
                ids = [lists[2 * slots + o * capf + e * capb + s] for s in range(capb)]
                rhs = jnp.concatenate([xg[j][i] for i in ids], axis=0)
                res = jnp.dot(v.dense[o * kparts + e], rhs, preferred_element_type=F32)
                total = res if total is None else total + res
            total = total.astype(BF)
            if j == 0:
                v.pa[pl.ds(o * npa, npa)] = total.reshape(npa, arows, wf[j])
            else:
                v.pb[pl.ds(o * npb, npb)] = total.reshape(npb, piece, wf[j])

    def backward(g, o):
        ids = [lists[5 * slots + o * capb + s] for s in range(capb)]
        rhs = jnp.concatenate([sp[g][i] for i in ids], axis=0)
        grads[g][o] = jnp.dot(v.dense[o], rhs, preferred_element_type=F32).astype(BF)


    def chain(part, acc, count, send, recv, to, shift, d, j, first):
        at = (d + shift) * count + j
        src = part.at[d * count + j] if first else acc.at[at]
        return remote(src, acc.at[at], send.at[shift, d], recv.at[d + shift, j], to)

    def group(part, acc, count, send, recv):
        def cp_r(d, j, first=False):
            return chain(part, acc, count, send, recv, right, 1, d, j, first)

        def cp_l(d, j, first=False):
            return chain(part, acc, count, send, recv, left, 0, d, j, first)

        def hop(cp, shift, start, d, j):
            @pl.when(start)
            def _():
                cp(d, j, True).start()

            @pl.when(jnp.logical_not(start))
            def _():
                cp(d, j).wait_recv()
                at = (d + shift) * count + j
                acc[at] = (acc[at].astype(F32) + part[d * count + j].astype(F32)).astype(BF)
                cp(d, j).start()

        def live(j):
            return jnp.logical_and(j >= 0, j < count)

        def reduce_step(t):
            jr, jl = t - HOP * q, t - HOP * (last - q)

            @pl.when(live(jr))
            def _():
                @pl.loop(0, last - q)
                def _(i):
                    hop(cp_r, 1, q == 0, last - i, jr)

            @pl.when(live(jl))
            def _():
                @pl.loop(0, q)
                def _(i):
                    hop(cp_l, 0, q == last, i, jl)

        def total(j, buf):
            buf[...] = part[q * count + j].astype(F32)

            @pl.when(q > 0)
            def _():
                cp_r(q, j).wait_recv()
                buf[...] += acc[(q + 1) * count + j].astype(F32)

            @pl.when(q < last)
            def _():
                cp_l(q, j).wait_recv()
                buf[...] += acc[q * count + j].astype(F32)

        def sent():
            for d in range(n):
                ref = part.at[pl.ds(d * count, count)]

                @pl.when(q < d)
                def _():
                    remote(ref, ref, send.at[1, d], recv.at[0, 0], right).wait_send()

                @pl.when(q > d)
                def _():
                    remote(ref, ref, send.at[0, d], recv.at[0, 0], left).wait_send()

        return types.SimpleNamespace(live=live, reduce_step=reduce_step, total=total, sent=sent)

    ga = group(v.pa, v.acca, npa, v.s_ra, v.r_ra)
    gb = group(v.pb, v.accb, npb, v.s_rb, v.r_rb)


    def part_of(d, j):
        at = d * npb + j
        return at // ppb, pl.ds(pl.multiple_of((at % ppb) * piece, piece), piece)

    def cp_g(side, to, d, j):
        b, at = part_of(d, j)
        ref = sp[0].at[b, at]
        return remote(ref, ref, v.s_g.at[side, d], v.r_g.at[d, j], to)

    cp_gr = functools.partial(cp_g, 1, right)
    cp_gl = functools.partial(cp_g, 0, left)

    def cp_h(g, side, to, d, h):
        ref = sp[g].at[pl.ds(d * nb + h * hb, hb)]
        return remote(ref, ref, v.s_h.at[g, side, d], v.r_h.at[g, d, h], to)

    def cp_hr(g):
        return functools.partial(cp_h, g, 1, right)

    def cp_hl(g):
        return functools.partial(cp_h, g, 0, left)

    def send_both(cr, cl, d, j):
        @pl.when(q < last)
        def _():
            cr(d, j).start()

        @pl.when(q > 0)
        def _():
            cl(d, j).start()

    def relay_on(cr, cl, ok, j, o):
        @pl.when(jnp.logical_and(ok, q >= o))
        def _():
            cr(q - o, j).wait_recv()

            @pl.when(q < last)
            def _():
                cr(q - o, j).start()

        @pl.when(jnp.logical_and(ok, q + o <= last))
        def _():
            cl(q + o, j).wait_recv()

            @pl.when(q > 0)
            def _():
                cl(q + o, j).start()

    def own_rest(g):
        for h in range(2):
            send_both(cp_hr(g), cp_hl(g), q, h)

    def relay_rest(g, o):
        for h in range(2):
            relay_on(cp_hr(g), cp_hl(g), True, h, o)

    def sent_on(g):
        send = v.s_g if g == 0 else v.s_h.at[g]
        recv = v.r_g.at[0, 0]
        for d in range(n):
            ref = sp[g].at[pl.ds(d * nb, nb)]

            @pl.when(jnp.logical_and(q >= d, q < last))
            def _():
                remote(ref, ref, send.at[1, d], recv, right).wait_send()

            @pl.when(jnp.logical_and(q <= d, q > 0))
            def _():
                remote(ref, ref, send.at[0, d], recv, left).wait_send()

    def finish_a(j):
        ga.total(j, v.fa)
        v.agg[pl.ds(pl.multiple_of(j * arows, arows), arows), : wf[0]] = v.fa[...].astype(BF)

    def finish(j):
        gb.total(j, v.fb)
        at = pl.ds(pl.multiple_of(j * piece, piece), piece)
        v.agg[at, wf[0] :] = v.fb[...].astype(BF)
        pre = jnp.dot(v.agg[at, :], w[...], preferred_element_type=F32) + bias[...]
        sig = jax.nn.sigmoid(pre)
        v.out[at, :] = (pre * sig).astype(BF)
        grad = (cot[at, :].astype(F32) * sig * (1.0 + pre * (1.0 - sig))).astype(BF)
        v.gp[at, :] = grad
        res = lax.dot_general(
            grad, w[...], (((1,), (1,)), ((), ())), preferred_element_type=F32
        ).astype(BF)
        b, sub = part_of(q, j)
        for g in range(ng):
            sp[g][b, sub, :] = res[:, sum(wb[:g]) : sum(wb[: g + 1])]
        send_both(cp_gr, cp_gl, q, j)


    cp_w1 = remote(v.wp.at[1 - c], v.w1, v.s_w.at[0], v.r_w.at[0], partner)
    w4 = v.w4

    def cp_w2(d):
        return remote(v.w1.at[flip(k, d)], v.w2.at[d - 1], v.s_w.at[1], v.r_w.at[1], dev(d))

    def cp_w3(dz):
        return remote(v.ws, v.w3.at[dz - 1], v.s_w.at[2], v.r_w.at[2], deep(dz))

    def cp_w4(d):
        return remote(w4.at[c, k], w4.at[c, k], v.s_w.at[3], v.r_w.at[3], dev(d))

    def cp_w5(d):
        ref = w4.at[c, flip(k, d)]
        return remote(ref, ref, v.s_w.at[4], v.r_w.at[4], partner)

    def all_w(ref, i):
        return remote(ref, ref, v.s_w.at[i], v.r_w.at[i], partner)

    all_w2 = all_w(v.w2, 1)
    all_w3 = all_w(v.w3, 2)
    all_w4 = all_w(w4.at[0, pl.ds(0, chips - 1)], 3)
    all_w5 = all_w(w4.at[0], 4)

    def weight_1():
        cp_w1.wait_recv()
        for z in range(chips):
            v.w1[z] = (v.w1[z].astype(F32) + v.wp[c, z].astype(F32)).astype(BF)
        for d in range(1, chips):
            cp_w2(d).start()

    def weight_2():
        all_w2.wait_recv()
        total = v.w1[k].astype(F32)
        for d in range(1, chips):
            total = total + v.w2[d - 1].astype(F32)
        v.ws[...] = total.astype(BF)
        for dz in range(1, n):
            cp_w3(dz).start()

    def weight_3():
        all_w3.wait_recv()
        total = None
        for i in range(n):
            other = v.w3[jnp.maximum((q - i + n) % n - 1, 0)].astype(F32)
            term = jnp.where(q == i, v.ws[...].astype(F32), other)
            total = term if total is None else total + term
        w4[c, k] = total.astype(BF)
        for d in range(1, chips):
            cp_w4(d).start()
        cp_w5(0).start()

    def weight_4():
        all_w4.wait_recv()
        for d in range(1, chips):
            cp_w5(d).start()

    store_w = pltpu.make_async_copy(w4, wg, v.s_load.at[1])

    def weight_5():
        all_w5.wait_recv()
        bg[...] = w4[0, 0, w4.shape[2] - PAD :, :].astype(F32)[:1]
        store_w.start()

    def weight_sent():
        cp_w1.wait_send()
        for a in (all_w2, all_w3, all_w4, all_w5):
            a.wait_send()
        store_w.wait()


    half = rows // 2

    def mine(g, d):
        return grads[g].at[flip(k, d) * 2 + c]

    def cp_a(g, d):
        return remote(
            grads[g].at[flip(k, d) * 2 + 1 - c],
            abuf[g].at[d],
            v.s_a.at[g],
            v.r_a.at[g, d],
            partner,
        )

    def cp_b(g, d, h):
        at = pl.ds(h * half, half)
        i = near.index(d)
        return remote(abuf[g].at[d, at], bbuf[g].at[i, at], v.s_b.at[g], v.r_b.at[g], dev(d))

    def all_b(g):
        return remote(bbuf[g], bbuf[g], v.s_b.at[g], v.r_b.at[g], partner)

    def cp_c(g, h):
        return remote(
            abuf[g].at[3, pl.ds(h * half, half)],
            cbuf[g].at[h],
            v.s_c.at[g],
            v.r_c.at[g, h],
            dev(h + 1),
        )

    def join(g, d):
        cp_a(g, d).wait_recv()
        add_rows(abuf[g].at[d], [abuf[g].at[d], mine(g, d)], 0, rows)

    def products(g):
        @pl.loop(0, chips)
        def _(i):
            d = chips - 1 - i
            at = flip(k, d) * 2
            backward(g, at + 1 - c)
            cp_a(g, d).start()
            backward(g, at + c)

    def rows_1(g):
        if relay:
            join(g, 3)
            cp_c(g, 0).start()
            cp_c(g, 1).start()
            join(g, 2)
            cp_b(g, 2, 1).start()
            join(g, 1)
            cp_b(g, 1, 0).start()
        else:
            for d in range(chips - 1, 0, -1):
                join(g, d)
                for h in range(2):
                    cp_b(g, d, h).start()

    def rows_2(g):
        if relay:
            cp_c(g, 0).wait_recv()
            add_rows(abuf[g].at[2], [abuf[g].at[2], cbuf[g].at[0]], 0, half)
            cp_b(g, 2, 0).start()
            cp_c(g, 1).wait_recv()
            at = pl.ds(half, half)
            add_rows(abuf[g].at[1, at], [abuf[g].at[1, at], cbuf[g].at[1]], 0, half)
            cp_b(g, 1, 1).start()
        join(g, 0)

    def store(g):
        return pltpu.make_async_copy(
            fgs[g], fg.at[:, pl.ds(sum(wb[:g]), wb[g])], v.s_store.at[g]
        )

    def rows_3(g):
        all_b(g).wait_recv()
        add_rows(fgs[g], [abuf[g].at[0]] + [bbuf[g].at[i] for i in range(len(near))], 0, rows)
        store(g).start()

    def rows_sent(g):
        remote(
            grads[g].at[pl.ds(0, chips)], abuf[g], v.s_a.at[g], v.r_a.at[g, 0], partner
        ).wait_send()
        all_b(g).wait_send()
        if relay:
            remote(cbuf[g], cbuf[g], v.s_c.at[g], v.r_c.at[g, 0], partner).wait_send()
        store(g).wait()


    barrier = pltpu.get_barrier_semaphore()
    peers = [partner] + [dev(d) for d in range(1, chips)] + [deep(dz) for dz in range(1, n)]
    for peer in peers:
        pl.semaphore_signal(barrier, inc=1, device_id=peer, device_id_type=MESH)
    loads = [
        pltpu.make_async_copy(a, b, v.s_load.at[i])
        for i, (a, b) in enumerate([(tiles_in, v.tiles), (w_in, w), (cot_in, cot)])
    ]
    store_out = pltpu.make_async_copy(v.out, out, v.s_load.at[0])
    for j in range(nch):
        take(j).start()
    for load in loads:
        load.start()
    pl.semaphore_wait(barrier, len(peers))

    gather_start(0)
    for load in loads:
        load.wait()

    @pl.loop(0, n)
    def _(o):
        build(o, 0, capf, False)

    gather_mid(0)
    gather_start(1)
    gather_end(0)
    forward(0)
    ga.reduce_step(0)
    gather_mid(1)
    ga.reduce_step(1)
    gather_end(1)
    ga.reduce_step(2)
    forward(1)

    begin = 3
    wait = HOP * last
    done = npa + npb + wait - 1

    @pl.loop(begin, npa + npb + wait + RING * last)
    def _(t):
        ga.reduce_step(t)
        gb.reduce_step(t - npa)

        for e in range(npa):
            @pl.when(t == max(begin, wait + e))
            def _():
                finish_a(e)

        j = t - npa - wait

        @pl.when(gb.live(j))
        def _():
            finish(j)

        for o in range(1, n):
            p = j - RING * o
            relay_on(cp_gr, cp_gl, gb.live(p), p, o)

        o = t - begin

        @pl.when(jnp.logical_and(o >= 0, o < nrow))
        def _():
            build(o, 3, capb, True)

        @pl.when(t == done)
        def _():
            for g in range(1, ng):
                own_rest(g)
            store_out.start()
            weight_block(chips, scale, v.agg, v.gp, v.wp)
            cp_w1.start()

    for g in range(1, ng):
        relay_rest(g, 1)
    products(0)
    relay_rest(1, 2)
    rows_1(0)
    weight_1()
    relay_rest(2, 2)
    for o in range(3, n):
        relay_rest(1, o)
    products(1)
    rows_2(0)
    rows_1(1)
    weight_2()
    for o in range(3, n):
        relay_rest(2, o)
    products(2)
    rows_1(2)
    weight_3()
    rows_3(0)
    rows_2(1)
    weight_4()
    rows_2(2)
    rows_3(1)
    weight_5()
    rows_3(2)

    for j in range(nch):
        gather_sent(j)
    ga.sent()
    gb.sent()
    for g in range(ng):
        sent_on(g)
    for g in range(ng):
        rows_sent(g)
    weight_sent()
    store_out.wait()


def tail_kernel(out_in, fg_in, parts, bg_in, out, fg, wg, bg):
    out[...] = out_in[...]
    fg[...] = fg_in[...]
    chips = parts.shape[1]
    rows = wg.shape[0] // (2 * chips)
    for a in range(2):
        for b in range(chips):
            at = (a * chips + b) * rows
            wg[at : at + rows, :] = parts[a, b, :rows, :].astype(F32)
    bg[...] = bg_in[...]


VM = pl.BlockSpec(memory_space=pltpu.VMEM)
SM = pl.BlockSpec(memory_space=pltpu.SMEM)
ANY = pl.BlockSpec(memory_space=pl.ANY)


def dma(*shape):
    return pltpu.SemaphoreType.DMA(shape)


def on_device(features, weight, bias, cotangent, tile_values, tile_rows, tile_cols, tile_counts):
    nrow = lax.axis_size("row")
    ncol = lax.axis_size("col")
    node_dev, width = features.shape
    slots, size = tile_values.shape[2], tile_values.shape[3]
    nb = node_dev // size
    chips = nrow // 2
    scale = 1.0 / math.sqrt(node_dev * nrow * ncol)
    values = tile_values.reshape(slots, size, size)

    lists = pl.pallas_call(
        functools.partial(list_kernel, nrow, ncol, nb),
        out_shape=jax.ShapeDtypeStruct((LISTS * slots,), jnp.int32),
        in_specs=[SM, SM, SM],
        out_specs=SM,
        scratch_shapes=[pltpu.SMEM((nrow + ncol,), jnp.int32)],
        name="lists",
    )(tile_counts.reshape(1), tile_rows.reshape(slots), tile_cols.reshape(slots))

    wf = (width // 2, width - width // 2)
    wb = (width // 2, width // 4, width - width // 2 - width // 4)
    nch, ng = len(wf), len(wb)
    npa = 4
    arows = node_dev // npa
    piece = size // 2
    npb = node_dev // piece
    pr = width // (2 * chips) + PAD
    capb = slots // nrow

    def vm(*shape, dtype=BF):
        return pltpu.VMEM(shape, dtype)

    scratch = {"x%d" % j: vm(nrow * nb, size, wf[j]) for j in range(nch)}
    scratch.update(
        tiles=vm(slots, size, size),
        dense=vm(nrow, node_dev, capb * size),
        pa=vm(ncol * npa, arows, wf[0]),
        pb=vm(ncol * npb, piece, wf[1]),
        acca=vm((ncol + 1) * npa, arows, wf[0]),
        accb=vm((ncol + 1) * npb, piece, wf[1]),
        fa=vm(arows, wf[0], dtype=F32),
        fb=vm(piece, wf[1], dtype=F32),
        w=vm(width, width),
        cot=vm(node_dev, width),
        agg=vm(node_dev, width),
        gp=vm(node_dev, width),
        wp=vm(2, chips, pr, width),
        w1=vm(chips, pr, width),
        w2=vm(chips - 1, pr, width),
        w3=vm(ncol - 1, pr, width),
        w4=vm(2, chips, pr, width),
        out=vm(node_dev, width),
        ws=vm(pr, width),
        s_take=dma(nch),
        s_load=dma(3),
        s_same=dma(nch),
        r_same=dma(nch, chips, 2),
        s_part=dma(nch),
        r_part=dma(nch),
        s_ra=dma(2, ncol),
        r_ra=dma(ncol + 1, npa),
        s_rb=dma(2, ncol),
        r_rb=dma(ncol + 1, npb),
        s_g=dma(2, ncol),
        r_g=dma(ncol, npb),
        s_h=dma(ng, 2, ncol),
        r_h=dma(ng, ncol, 2),
        s_a=dma(ng),
        r_a=dma(ng, chips),
        s_b=dma(ng),
        r_b=dma(ng),
        s_c=dma(ng),
        r_c=dma(ng, 2),
        s_w=dma(5),
        r_w=dma(5),
        s_store=dma(ng),
    )
    others = chips - 1 - (chips == 4)
    for g in range(ng):
        scratch["sp%d" % g] = vm(ncol * nb, size, wb[g])
        scratch["g%d" % g] = vm(nrow, node_dev, wb[g])
        scratch["a%d" % g] = vm(chips, node_dev, wb[g])
        scratch["b%d" % g] = vm(others, node_dev, wb[g])
        scratch["c%d" % g] = vm(2, node_dev // 2, wb[g])
        scratch["f%d" % g] = vm(node_dev, wb[g])

    out, fg, parts, bg = pl.pallas_call(
        functools.partial(mega_kernel, tuple(scratch), ncol, nrow, nb, scale, wf, wb),
        out_shape=[
            jax.ShapeDtypeStruct((node_dev, width), BF),
            jax.ShapeDtypeStruct((node_dev, width), BF),
            jax.ShapeDtypeStruct((2, chips, pr, width), BF),
            jax.ShapeDtypeStruct((1, width), F32),
        ],
        in_specs=[SM, ANY, ANY, ANY, VM, ANY],
        out_specs=[ANY, ANY, ANY, VM],
        scratch_shapes=list(scratch.values()),
        compiler_params=pltpu.CompilerParams(
            collective_id=0, has_side_effects=True, vmem_limit_bytes=60 << 20
        ),
        name="layer",
    )(
        lists,
        features.reshape(nb, size, width),
        values,
        weight,
        bias.reshape(1, width),
        cotangent,
    )

    out, fg, wg, bg = pl.pallas_call(
        tail_kernel,
        out_shape=[
            jax.ShapeDtypeStruct((node_dev, width), BF),
            jax.ShapeDtypeStruct((node_dev, width), BF),
            jax.ShapeDtypeStruct((width, width), F32),
            jax.ShapeDtypeStruct((1, width), F32),
        ],
        in_specs=[VM] * 4,
        out_specs=[VM] * 4,
        name="tail",
    )(out, fg, parts, bg)
    return (out, fg, wg, bg.reshape(width))


def solution(mesh):
    return jax.shard_map(
        on_device,
        mesh=mesh,
        in_specs=(
            P(("row", "col"), None),
            P(),
            P(),
            P(("row", "col"), None),
            P("row", "col", None, None, None),
            P("row", "col", None),
            P("row", "col", None),
            P("row", "col"),
        ),
        out_specs=(P(("row", "col"), None), P(("row", "col"), None), P(), P()),
        check_vma=False,
    )
```

```python
import functools
import math
import types

import jax
import jax.numpy as jnp
from jax import lax
from jax.experimental import pallas as pl
from jax.experimental.pallas import tpu as pltpu
from jax.sharding import PartitionSpec as P

MESH = pl.DeviceIdType.MESH
BF = jnp.bfloat16
F32 = jnp.float32
PAD = 16
PARTS = 4
HOP = 1
RING = 1
LISTS = 6


def flip(k, d):
    out = 0
    for b in range(8):
        step = 1 << b
        if isinstance(d, int):
            if d < step:
                bit = 0
            else:
                bit = (d // step) % 2
        else:
            bit = (d // step) % 2
        kb = (k // step) % 2
        if isinstance(bit, int):
            out = out + step * ((1 - kb) if bit else kb)
        else:
            out = out + step * (kb + bit - 2 * kb * bit)
    return out


def remote(src, dst, send, recv, to):
    return pltpu.make_async_remote_copy(
        src_ref=src, dst_ref=dst, send_sem=send, recv_sem=recv, device_id=to, device_id_type=MESH
    )


def list_kernel(nrow, ncol, blk, counts, rows, cols, out, lens):
    slots = rows.shape[0]
    capf, capb = slots // ncol, slots // nrow
    span = blk * ncol

    @pl.loop(0, slots)
    def _(i):
        out[i] = 0
        out[slots + i] = -1
        out[2 * slots + i] = 0
        out[3 * slots + i] = 0
        out[4 * slots + i] = -1
        out[5 * slots + i] = 0

    @pl.loop(0, nrow + ncol)
    def _(i):
        lens[i] = 0

    @pl.loop(0, counts[0])
    def _(k):
        row = rows[k] % span
        col = cols[k]
        o = row // blk
        at = o * capf + lens[o]
        lens[o] = lens[o] + 1
        dev = col // span
        src = dev * blk + col % blk
        out[at] = k
        out[slots + at] = row % blk
        out[2 * slots + at] = src
        bt = dev * capb + lens[ncol + dev]
        lens[ncol + dev] = lens[ncol + dev] + 1
        out[3 * slots + bt] = k
        out[4 * slots + bt] = col % blk
        out[5 * slots + bt] = row


def add_rows(dst, srcs, begin, count):
    step = 64

    @pl.loop(0, count // step)
    def _(i):
        at = pl.ds(pl.multiple_of(begin + i * step, step), step)
        total = srcs[0][at, :].astype(F32)
        for s in srcs[1:]:
            total = total + s[at, :].astype(F32)
        dst[at, :] = total.astype(dst.dtype)


def weight_block(parts, scale, agg, gp, wp):
    width = agg.shape[1]
    rows = width // (2 * parts)
    total = jnp.sum(gp[...].astype(F32), axis=0, keepdims=True) * scale
    pad = jnp.broadcast_to(total, (PAD, width)).astype(BF)
    step = 128
    for t in range(width // step):
        res = lax.dot_general(
            agg[:, t * step : (t + 1) * step],
            gp[...],
            (((0,), (0,)), ((), ())),
            preferred_element_type=F32,
        )
        res = (res * scale).astype(BF)
        for u in range(step // rows):
            p = (t * step) // rows + u
            wp[p // parts, p % parts, :rows, :] = res[u * rows : (u + 1) * rows]
            wp[p // parts, p % parts, rows:, :] = pad


def mega_kernel(
    names, n, nrow, nb, scale, wf, wb, lists, feats, tiles_in, w_in, bias, cot_in, out, fg, wg, bg,
    *scratch
):
    v = types.SimpleNamespace(**dict(zip(names, scratch)))
    r, q = lax.axis_index("row"), lax.axis_index("col")
    k, c = r // 2, r % 2
    chips = nrow // 2
    last = n - 1
    right, left = (r, jnp.minimum(q + 1, last)), (r, jnp.maximum(q - 1, 0))
    partner = (k * 2 + 1 - c, q)
    relay = chips == 4
    near = [d for d in range(1, chips) if not (relay and d == 3)]
    hb = nb // 2
    slots, size = v.tiles.shape[0], v.tiles.shape[1]
    rows = nb * size
    capf, capb = slots // n, slots // nrow
    kparts = capf // capb
    nch, ng = len(wf), len(wb)
    w, cot = v.w, v.cot
    npa = v.pa.shape[0] // n
    arows = rows // npa
    npb = v.pb.shape[0] // n
    piece = rows // npb
    ppb = size // piece
    xg = [getattr(v, "x%d" % j) for j in range(nch)]
    sp, grads, abuf, bbuf, cbuf, fgs = (
        [getattr(v, "%s%d" % (name, g)) for g in range(ng)]
        for name in ("sp", "g", "a", "b", "c", "f")
    )

    def dev(d):
        return (flip(k, d) * 2 + c, q)

    def deep(dz):
        return (r, (q + dz) % n)


    def take(j):
        return pltpu.make_async_copy(
            feats.at[:, :, pl.ds(sum(wf[:j]), wf[j])], xg[j].at[pl.ds(r * nb, nb)], v.s_take.at[j]
        )

    def slot(j, d, core, h):
        return xg[j].at[pl.ds((flip(k, d) * 2 + core) * nb + h * hb, hb)]

    def same(j, d, h, to, at):
        ref = slot(j, d, c, h)
        return remote(ref, ref, v.s_same.at[j], v.r_same.at[j, at, h], dev(to))

    def own(j, d, h):
        return same(j, 0, h, d, d)

    def pass_on(j, h):
        via, to = (1, 2) if h == 0 else (2, 1)
        return same(j, via, h, to, 3)

    def inc(j, d, h):
        return same(j, d, h, d, d)

    def fwd(j, d, h):
        ref = slot(j, d, c, h)
        return remote(ref, ref, v.s_part.at[j], v.r_part.at[j], partner)

    def gather_start(j):
        take(j).wait()
        for i in range(2):
            for d in near:
                own(j, d, (i + (d == 2)) % 2).start()
        for h in range(2):
            fwd(j, 0, h).start()

    def gather_mid(j):
        for i in range(2):
            for d in near:
                h = (i + (d == 2)) % 2
                inc(j, d, h).wait_recv()
                if relay and i == 0:
                    pass_on(j, h).start()
                fwd(j, d, h).start()

    def whole(j, count):
        ref = xg[j].at[pl.ds(0, count * nb)]
        return remote(ref, ref, v.s_part.at[j], v.r_part.at[j], partner)

    def gather_end(j):
        if relay:
            for h in range(2):
                inc(j, 3, h).wait_recv()
                fwd(j, 3, h).start()
        whole(j, chips).wait_recv()

    def gather_sent(j):
        ref = xg[j].at[pl.ds(0, (chips - 1) * nb)]
        remote(ref, ref, v.s_same.at[j], v.r_same.at[j, 0, 0], partner).wait_send()
        whole(j, chips).wait_send()


    def build(o, base, cap, back):
        for s in range(cap):
            at = o * cap + s
            mat = v.tiles[lists[base * slots + at]]
            place = lists[(base + 1) * slots + at]
            if back:
                mat = jnp.transpose(mat)
            for b in range(nb):
                val = jnp.where(place == b, mat, jnp.zeros_like(mat))
                if back:
                    v.dense[o, b * size : (b + 1) * size, s * size : (s + 1) * size] = val
                else:
                    u = s % capb
                    v.dense[
                        o * kparts + s // capb, b * size : (b + 1) * size, u * size : (u + 1) * size
                    ] = val

    def forward(j):
        @pl.loop(0, n)
        def _(o):
            total = None
            for e in range(kparts):
                ids = [lists[2 * slots + o * capf + e * capb + s] for s in range(capb)]
                rhs = jnp.concatenate([xg[j][i] for i in ids], axis=0)
                res = jnp.dot(v.dense[o * kparts + e], rhs, preferred_element_type=F32)
                total = res if total is None else total + res
            total = total.astype(BF)
            if j == 0:
                v.pa[pl.ds(o * npa, npa)] = total.reshape(npa, arows, wf[j])
            else:
                v.pb[pl.ds(o * npb, npb)] = total.reshape(npb, piece, wf[j])

    def backward(g, o):
        ids = [lists[5 * slots + o * capb + s] for s in range(capb)]
        rhs = jnp.concatenate([sp[g][i] for i in ids], axis=0)
        grads[g][o] = jnp.dot(v.dense[o], rhs, preferred_element_type=F32).astype(BF)


    def chain(part, acc, count, send, recv, to, shift, d, j, first):
        at = (d + shift) * count + j
        src = part.at[d * count + j] if first else acc.at[at]
        return remote(src, acc.at[at], send.at[shift, d], recv.at[d + shift, j], to)

    def group(part, acc, count, send, recv):
        def cp_r(d, j, first=False):
            return chain(part, acc, count, send, recv, right, 1, d, j, first)

        def cp_l(d, j, first=False):
            return chain(part, acc, count, send, recv, left, 0, d, j, first)

        def hop(cp, shift, start, d, j):
            @pl.when(start)
            def _():
                cp(d, j, True).start()

            @pl.when(jnp.logical_not(start))
            def _():
                cp(d, j).wait_recv()
                at = (d + shift) * count + j
                acc[at] = (acc[at].astype(F32) + part[d * count + j].astype(F32)).astype(BF)
                cp(d, j).start()

        def live(j):
            return jnp.logical_and(j >= 0, j < count)

        def reduce_step(t):
            jr, jl = t - HOP * q, t - HOP * (last - q)

            @pl.when(live(jr))
            def _():
                @pl.loop(0, last - q)
                def _(i):
                    hop(cp_r, 1, q == 0, last - i, jr)

            @pl.when(live(jl))
            def _():
                @pl.loop(0, q)
                def _(i):
                    hop(cp_l, 0, q == last, i, jl)

        def total(j, buf):
            buf[...] = part[q * count + j].astype(F32)

            @pl.when(q > 0)
            def _():
                cp_r(q, j).wait_recv()
                buf[...] += acc[(q + 1) * count + j].astype(F32)

            @pl.when(q < last)
            def _():
                cp_l(q, j).wait_recv()
                buf[...] += acc[q * count + j].astype(F32)

        def sent():
            for d in range(n):
                ref = part.at[pl.ds(d * count, count)]

                @pl.when(q < d)
                def _():
                    remote(ref, ref, send.at[1, d], recv.at[0, 0], right).wait_send()

                @pl.when(q > d)
                def _():
                    remote(ref, ref, send.at[0, d], recv.at[0, 0], left).wait_send()

        return types.SimpleNamespace(live=live, reduce_step=reduce_step, total=total, sent=sent)

    ga = group(v.pa, v.acca, npa, v.s_ra, v.r_ra)
    gb = group(v.pb, v.accb, npb, v.s_rb, v.r_rb)


    def part_of(d, j):
        at = d * npb + j
        return at // ppb, pl.ds(pl.multiple_of((at % ppb) * piece, piece), piece)

    def cp_g(side, to, d, j):
        b, at = part_of(d, j)
        ref = sp[0].at[b, at]
        return remote(ref, ref, v.s_g.at[side, d], v.r_g.at[d, j], to)

    cp_gr = functools.partial(cp_g, 1, right)
    cp_gl = functools.partial(cp_g, 0, left)

    def cp_h(g, side, to, d, h):
        ref = sp[g].at[pl.ds(d * nb + h * hb, hb)]
        return remote(ref, ref, v.s_h.at[g, side, d], v.r_h.at[g, d, h], to)

    def cp_hr(g):
        return functools.partial(cp_h, g, 1, right)

    def cp_hl(g):
        return functools.partial(cp_h, g, 0, left)

    def send_both(cr, cl, d, j):
        @pl.when(q < last)
        def _():
            cr(d, j).start()

        @pl.when(q > 0)
        def _():
            cl(d, j).start()

    def relay_on(cr, cl, ok, j, o):
        @pl.when(jnp.logical_and(ok, q >= o))
        def _():
            cr(q - o, j).wait_recv()

            @pl.when(q < last)
            def _():
                cr(q - o, j).start()

        @pl.when(jnp.logical_and(ok, q + o <= last))
        def _():
            cl(q + o, j).wait_recv()

            @pl.when(q > 0)
            def _():
                cl(q + o, j).start()

    def own_rest(g):
        for h in range(2):
            send_both(cp_hr(g), cp_hl(g), q, h)

    def relay_rest(g, o):
        for i in range(o, n if o == 3 else min(o + 1, n)):
            for h in range(2):
                relay_on(cp_hr(g), cp_hl(g), True, h, i)

    def sent_on(g):
        send = v.s_g if g == 0 else v.s_h.at[g]
        recv = v.r_g.at[0, 0]
        for d in range(n):
            ref = sp[g].at[pl.ds(d * nb, nb)]

            @pl.when(jnp.logical_and(q >= d, q < last))
            def _():
                remote(ref, ref, send.at[1, d], recv, right).wait_send()

            @pl.when(jnp.logical_and(q <= d, q > 0))
            def _():
                remote(ref, ref, send.at[0, d], recv, left).wait_send()

    def finish_a(j):
        ga.total(j, v.fa)
        v.agg[pl.ds(pl.multiple_of(j * arows, arows), arows), : wf[0]] = v.fa[...].astype(BF)

    def finish(j):
        gb.total(j, v.fb)
        at = pl.ds(pl.multiple_of(j * piece, piece), piece)
        v.agg[at, wf[0] :] = v.fb[...].astype(BF)
        pre = jnp.dot(v.agg[at, :], w[...], preferred_element_type=F32) + bias[...]
        sig = jax.nn.sigmoid(pre)
        v.out[at, :] = (pre * sig).astype(BF)
        grad = (cot[at, :].astype(F32) * sig * (1.0 + pre * (1.0 - sig))).astype(BF)
        v.gp[at, :] = grad
        res = lax.dot_general(
            grad, w[...], (((1,), (1,)), ((), ())), preferred_element_type=F32
        ).astype(BF)
        b, sub = part_of(q, j)
        for g in range(ng):
            sp[g][b, sub, :] = res[:, sum(wb[:g]) : sum(wb[: g + 1])]
        send_both(cp_gr, cp_gl, q, j)


    cp_w1 = remote(v.wp.at[1 - c], v.w1, v.s_w.at[0], v.r_w.at[0], partner)
    w4 = v.w4

    def cp_w2(dz):
        return remote(v.w1.at[(q + dz) % n], v.w2.at[dz - 1], v.s_w.at[1], v.r_w.at[1], deep(dz))

    def cp_w3(d):
        return remote(v.ws, v.w3.at[d - 1], v.s_w.at[2], v.r_w.at[2], dev(d))

    def cp_w4(dz):
        return remote(w4.at[c, q], w4.at[c, q], v.s_w.at[3], v.r_w.at[3], deep(dz))

    cp_w5 = remote(w4.at[c], w4.at[c], v.s_w.at[4], v.r_w.at[4], partner)

    def all_w(ref, i):
        return remote(ref, ref, v.s_w.at[i], v.r_w.at[i], partner)

    all_w2 = all_w(v.w2, 1)
    all_w3 = all_w(v.w3, 2)
    all_w4 = all_w(w4.at[0, pl.ds(0, n - 1)], 3)

    def weight_0():
        weight_block(n, scale, v.agg, v.gp, v.wp)
        cp_w1.start()

    def weight_1():
        cp_w1.wait_recv()
        for z in range(n):
            v.w1[z] = (v.w1[z].astype(F32) + v.wp[c, z].astype(F32)).astype(BF)
        for dz in range(1, n):
            cp_w2(dz).start()

    def weight_2():
        all_w2.wait_recv()
        total = v.w1[q].astype(F32)
        for dz in range(1, n):
            total = total + v.w2[dz - 1].astype(F32)
        v.ws[...] = total.astype(BF)
        for d in range(1, chips):
            cp_w3(d).start()

    def weight_3():
        all_w3.wait_recv()
        total = None
        for i in range(chips):
            other = v.w3[jnp.maximum(flip(k, i) - 1, 0)].astype(F32)
            term = jnp.where(k == i, v.ws[...].astype(F32), other)
            total = term if total is None else total + term
        w4[c, q] = total.astype(BF)
        for dz in range(1, n):
            cp_w4(dz).start()

    def weight_4():
        all_w4.wait_recv()
        cp_w5.start()

    store_w = pltpu.make_async_copy(w4, wg, v.s_load.at[1])

    def weight_5():
        remote(
            w4.at[1 - c], w4.at[1 - c], v.s_w.at[4], v.r_w.at[4], partner
        ).wait_recv()
        bg[...] = w4[0, 0, w4.shape[2] - PAD :, :].astype(F32)[:1]
        store_w.start()

    def weight_sent():
        cp_w1.wait_send()
        for a in (all_w2, all_w3, all_w4, cp_w5):
            a.wait_send()
        store_w.wait()


    half = rows // 2

    def mine(g, d):
        return grads[g].at[flip(k, d) * 2 + c]

    def cp_a(g, d):
        return remote(
            grads[g].at[flip(k, d) * 2 + 1 - c],
            abuf[g].at[d],
            v.s_a.at[g],
            v.r_a.at[g, d],
            partner,
        )

    def cp_b(g, d, h):
        at = pl.ds(h * half, half)
        i = near.index(d)
        return remote(abuf[g].at[d, at], bbuf[g].at[i, at], v.s_b.at[g], v.r_b.at[g], dev(d))

    def all_b(g):
        return remote(bbuf[g], bbuf[g], v.s_b.at[g], v.r_b.at[g], partner)

    def cp_c(g, h):
        return remote(
            abuf[g].at[3, pl.ds(h * half, half)],
            cbuf[g].at[h],
            v.s_c.at[g],
            v.r_c.at[g, h],
            dev(h + 1),
        )

    def join(g, d):
        cp_a(g, d).wait_recv()
        add_rows(abuf[g].at[d], [abuf[g].at[d], mine(g, d)], 0, rows)

    def pass_first(g, d):
        join(g, d)
        if not relay:
            for h in range(2):
                cp_b(g, d, h).start()
        elif d == 3:
            for h in range(2):
                cp_c(g, h).start()
        else:
            cp_b(g, d, d - 1).start()

    def products(g, part):
        for i in range(part * chips // PARTS, (part + 1) * chips // PARTS):
            d = chips - 1 - i
            at = flip(k, d) * 2
            backward(g, at + 1 - c)
            cp_a(g, d).start()
            backward(g, at + c)
            if i > 0:
                pass_first(g, d + 1)

    def rows_2(g):
        if relay:
            cp_c(g, 0).wait_recv()
            add_rows(abuf[g].at[2], [abuf[g].at[2], cbuf[g].at[0]], 0, half)
            cp_b(g, 2, 0).start()
            cp_c(g, 1).wait_recv()
            at = pl.ds(half, half)
            add_rows(abuf[g].at[1, at], [abuf[g].at[1, at], cbuf[g].at[1]], 0, half)
            cp_b(g, 1, 1).start()
        join(g, 0)

    def store(g):
        return pltpu.make_async_copy(
            fgs[g], fg.at[:, pl.ds(sum(wb[:g]), wb[g])], v.s_store.at[g]
        )

    def rows_3(g):
        all_b(g).wait_recv()
        add_rows(fgs[g], [abuf[g].at[0]] + [bbuf[g].at[i] for i in range(len(near))], 0, rows)
        store(g).start()

    def rows_sent(g):
        remote(
            grads[g].at[pl.ds(0, chips)], abuf[g], v.s_a.at[g], v.r_a.at[g, 0], partner
        ).wait_send()
        all_b(g).wait_send()
        if relay:
            remote(cbuf[g], cbuf[g], v.s_c.at[g], v.r_c.at[g, 0], partner).wait_send()
        store(g).wait()


    barrier = pltpu.get_barrier_semaphore()
    peers = [partner] + [dev(d) for d in range(1, chips)] + [deep(dz) for dz in range(1, n)]
    for peer in peers:
        pl.semaphore_signal(barrier, inc=1, device_id=peer, device_id_type=MESH)
    loads = [
        pltpu.make_async_copy(a, b, v.s_load.at[i])
        for i, (a, b) in enumerate([(tiles_in, v.tiles), (w_in, w), (cot_in, cot)])
    ]
    store_out = pltpu.make_async_copy(v.out, out, v.s_load.at[0])
    for j in range(nch):
        take(j).start()
    for load in loads:
        load.start()
    pl.semaphore_wait(barrier, len(peers))

    gather_start(0)
    for load in loads:
        load.wait()

    @pl.loop(0, n)
    def _(o):
        build(o, 0, capf, False)

    gather_mid(0)
    gather_start(1)
    gather_end(0)
    forward(0)
    ga.reduce_step(0)
    gather_mid(1)
    ga.reduce_step(1)
    gather_end(1)
    ga.reduce_step(2)
    forward(1)

    begin = 3
    wait = HOP * last
    done = npa + npb + wait - 1

    @pl.loop(begin, npa + npb + wait + RING * last)
    def _(t):
        ga.reduce_step(t)
        gb.reduce_step(t - npa)

        for e in range(npa):
            @pl.when(t == max(begin, wait + e))
            def _():
                finish_a(e)

        j = t - npa - wait

        @pl.when(gb.live(j))
        def _():
            finish(j)

        for o in range(1, n):
            p = j - RING * o
            relay_on(cp_gr, cp_gl, gb.live(p), p, o)

        o = t - begin

        @pl.when(jnp.logical_and(o >= 0, o < nrow))
        def _():
            build(o, 3, capb, True)

        @pl.when(t == done)
        def _():
            own_rest(1)
            own_rest(2)
            store_out.start()

    relay_rest(1, 1)
    products(0, 0)
    products(0, 1)
    weight_0()
    relay_rest(1, 2)
    relay_rest(2, 1)
    products(0, 2)
    relay_rest(2, 2)
    weight_1()
    relay_rest(1, 3)
    products(0, 3)
    rows_2(0)
    products(1, 0)
    products(1, 1)
    products(1, 2)
    rows_3(0)
    weight_2()
    relay_rest(2, 3)
    products(1, 3)
    rows_2(1)
    products(2, 0)
    weight_3()
    products(2, 1)
    products(2, 2)
    products(2, 3)
    rows_2(2)
    weight_4()
    rows_3(1)
    rows_3(2)
    weight_5()

    for j in range(nch):
        gather_sent(j)
    ga.sent()
    gb.sent()
    for g in range(ng):
        sent_on(g)
    for g in range(ng):
        rows_sent(g)
    weight_sent()
    store_out.wait()


def tail_kernel(out_in, fg_in, parts, bg_in, out, fg, wg, bg):
    out[...] = out_in[...]
    fg[...] = fg_in[...]
    count = parts.shape[1]
    rows = wg.shape[0] // (2 * count)
    for a in range(2):
        for b in range(count):
            at = (a * count + b) * rows
            wg[at : at + rows, :] = parts[a, b, :rows, :].astype(F32)
    bg[...] = bg_in[...]


VM = pl.BlockSpec(memory_space=pltpu.VMEM)
SM = pl.BlockSpec(memory_space=pltpu.SMEM)
ANY = pl.BlockSpec(memory_space=pl.ANY)


def dma(*shape):
    return pltpu.SemaphoreType.DMA(shape)


def on_device(features, weight, bias, cotangent, tile_values, tile_rows, tile_cols, tile_counts):
    nrow = lax.axis_size("row")
    ncol = lax.axis_size("col")
    node_dev, width = features.shape
    slots, size = tile_values.shape[2], tile_values.shape[3]
    nb = node_dev // size
    chips = nrow // 2
    scale = 1.0 / math.sqrt(node_dev * nrow * ncol)
    values = tile_values.reshape(slots, size, size)

    lists = pl.pallas_call(
        functools.partial(list_kernel, nrow, ncol, nb),
        out_shape=jax.ShapeDtypeStruct((LISTS * slots,), jnp.int32),
        in_specs=[SM, SM, SM],
        out_specs=SM,
        scratch_shapes=[pltpu.SMEM((nrow + ncol,), jnp.int32)],
        name="lists",
    )(tile_counts.reshape(1), tile_rows.reshape(slots), tile_cols.reshape(slots))

    wf = (width // 2, width - width // 2)
    wb = (width // 2, width // 4, width - width // 2 - width // 4)
    nch, ng = len(wf), len(wb)
    npa = 4
    arows = node_dev // npa
    piece = size // 2
    npb = node_dev // piece
    pr = width // (2 * ncol) + PAD
    capb = slots // nrow

    def vm(*shape, dtype=BF):
        return pltpu.VMEM(shape, dtype)

    scratch = {"x%d" % j: vm(nrow * nb, size, wf[j]) for j in range(nch)}
    scratch.update(
        tiles=vm(slots, size, size),
        dense=vm(nrow, node_dev, capb * size),
        pa=vm(ncol * npa, arows, wf[0]),
        pb=vm(ncol * npb, piece, wf[1]),
        acca=vm((ncol + 1) * npa, arows, wf[0]),
        accb=vm((ncol + 1) * npb, piece, wf[1]),
        fa=vm(arows, wf[0], dtype=F32),
        fb=vm(piece, wf[1], dtype=F32),
        w=vm(width, width),
        cot=vm(node_dev, width),
        agg=vm(node_dev, width),
        gp=vm(node_dev, width),
        wp=vm(2, ncol, pr, width),
        w1=vm(ncol, pr, width),
        w2=vm(ncol - 1, pr, width),
        w3=vm(chips - 1, pr, width),
        w4=vm(2, ncol, pr, width),
        out=vm(node_dev, width),
        ws=vm(pr, width),
        s_take=dma(nch),
        s_load=dma(3),
        s_same=dma(nch),
        r_same=dma(nch, chips, 2),
        s_part=dma(nch),
        r_part=dma(nch),
        s_ra=dma(2, ncol),
        r_ra=dma(ncol + 1, npa),
        s_rb=dma(2, ncol),
        r_rb=dma(ncol + 1, npb),
        s_g=dma(2, ncol),
        r_g=dma(ncol, npb),
        s_h=dma(ng, 2, ncol),
        r_h=dma(ng, ncol, 2),
        s_a=dma(ng),
        r_a=dma(ng, chips),
        s_b=dma(ng),
        r_b=dma(ng),
        s_c=dma(ng),
        r_c=dma(ng, 2),
        s_w=dma(5),
        r_w=dma(5),
        s_store=dma(ng),
    )
    others = chips - 1 - (chips == 4)
    for g in range(ng):
        scratch["sp%d" % g] = vm(ncol * nb, size, wb[g])
        scratch["g%d" % g] = vm(nrow, node_dev, wb[g])
        scratch["a%d" % g] = vm(chips, node_dev, wb[g])
        scratch["b%d" % g] = vm(others, node_dev, wb[g])
        scratch["c%d" % g] = vm(2, node_dev // 2, wb[g])
        scratch["f%d" % g] = vm(node_dev, wb[g])

    out, fg, parts, bg = pl.pallas_call(
        functools.partial(mega_kernel, tuple(scratch), ncol, nrow, nb, scale, wf, wb),
        out_shape=[
            jax.ShapeDtypeStruct((node_dev, width), BF),
            jax.ShapeDtypeStruct((node_dev, width), BF),
            jax.ShapeDtypeStruct((2, ncol, pr, width), BF),
            jax.ShapeDtypeStruct((1, width), F32),
        ],
        in_specs=[SM, ANY, ANY, ANY, VM, ANY],
        out_specs=[ANY, ANY, ANY, VM],
        scratch_shapes=list(scratch.values()),
        compiler_params=pltpu.CompilerParams(
            collective_id=0, has_side_effects=True, vmem_limit_bytes=60 << 20
        ),
        name="layer",
    )(
        lists,
        features.reshape(nb, size, width),
        values,
        weight,
        bias.reshape(1, width),
        cotangent,
    )

    out, fg, wg, bg = pl.pallas_call(
        tail_kernel,
        out_shape=[
            jax.ShapeDtypeStruct((node_dev, width), BF),
            jax.ShapeDtypeStruct((node_dev, width), BF),
            jax.ShapeDtypeStruct((width, width), F32),
            jax.ShapeDtypeStruct((1, width), F32),
        ],
        in_specs=[VM] * 4,
        out_specs=[VM] * 4,
        name="tail",
    )(out, fg, parts, bg)
    return (out, fg, wg, bg.reshape(width))


def solution(mesh):
    return jax.shard_map(
        on_device,
        mesh=mesh,
        in_specs=(
            P(("row", "col"), None),
            P(),
            P(),
            P(("row", "col"), None),
            P("row", "col", None, None, None),
            P("row", "col", None),
            P("row", "col", None),
            P("row", "col"),
        ),
        out_specs=(P(("row", "col"), None), P(("row", "col"), None), P(), P()),
        check_vma=False,
    )
```

```python
import functools
import math
import types

import jax
import jax.numpy as jnp
from jax import lax
from jax.experimental import pallas as pl
from jax.experimental.pallas import tpu as pltpu
from jax.sharding import PartitionSpec as P

MESH = pl.DeviceIdType.MESH
BF = jnp.bfloat16
F32 = jnp.float32
PAD = 16
PARTS = 4
HOP = 1
RING = 1
LISTS = 6


def flip(k, d):
    out = 0
    for b in range(8):
        step = 1 << b
        if isinstance(d, int):
            if d < step:
                bit = 0
            else:
                bit = (d // step) % 2
        else:
            bit = (d // step) % 2
        kb = (k // step) % 2
        if isinstance(bit, int):
            out = out + step * ((1 - kb) if bit else kb)
        else:
            out = out + step * (kb + bit - 2 * kb * bit)
    return out


def remote(src, dst, send, recv, to):
    return pltpu.make_async_remote_copy(
        src_ref=src, dst_ref=dst, send_sem=send, recv_sem=recv, device_id=to, device_id_type=MESH
    )


def list_kernel(nrow, ncol, blk, counts, rows, cols, out, lens):
    slots = rows.shape[0]
    capf, capb = slots // ncol, slots // nrow
    span = blk * ncol

    @pl.loop(0, slots, unroll=8)
    def _(i):
        out[i] = 0
        out[slots + i] = -1
        out[2 * slots + i] = 0
        out[3 * slots + i] = 0
        out[4 * slots + i] = -1
        out[5 * slots + i] = 0

    @pl.loop(0, nrow + ncol)
    def _(i):
        lens[i] = 0

    @pl.loop(0, counts[0])
    def _(k):
        row = rows[k] % span
        col = cols[k]
        o = row // blk
        at = o * capf + lens[o]
        lens[o] = lens[o] + 1
        dev = col // span
        src = dev * blk + col % blk
        out[at] = k
        out[slots + at] = row % blk
        out[2 * slots + at] = src
        bt = dev * capb + lens[ncol + dev]
        lens[ncol + dev] = lens[ncol + dev] + 1
        out[3 * slots + bt] = k
        out[4 * slots + bt] = col % blk
        out[5 * slots + bt] = row


def add_rows(dst, srcs, begin, count):
    step = 64

    @pl.loop(0, count // step)
    def _(i):
        at = pl.ds(pl.multiple_of(begin + i * step, step), step)
        total = srcs[0][at, :].astype(F32)
        for s in srcs[1:]:
            total = total + s[at, :].astype(F32)
        dst[at, :] = total.astype(dst.dtype)


def weight_block(parts, scale, agg, gp, wp):
    width = agg.shape[1]
    rows = width // (2 * parts)
    total = jnp.sum(gp[...].astype(F32), axis=0, keepdims=True) * scale
    pad = jnp.broadcast_to(total, (PAD, width)).astype(BF)
    step = 128
    for t in range(width // step):
        res = lax.dot_general(
            agg[:, t * step : (t + 1) * step],
            gp[...],
            (((0,), (0,)), ((), ())),
            preferred_element_type=F32,
        )
        res = (res * scale).astype(BF)
        for u in range(step // rows):
            p = (t * step) // rows + u
            wp[p // parts, p % parts, :rows, :] = res[u * rows : (u + 1) * rows]
            wp[p // parts, p % parts, rows:, :] = pad


def mega_kernel(
    names, n, nrow, nb, scale, wf, wb, lists, feats, tiles_in, w_in, bias, cot_in, out, fg, wg, bg,
    *scratch
):
    v = types.SimpleNamespace(**dict(zip(names, scratch)))
    r, q = lax.axis_index("row"), lax.axis_index("col")
    k, c = r // 2, r % 2
    chips = nrow // 2
    last = n - 1
    right, left = (r, jnp.minimum(q + 1, last)), (r, jnp.maximum(q - 1, 0))
    partner = (k * 2 + 1 - c, q)
    relay = chips == 4
    near = [d for d in range(1, chips) if not (relay and d == 3)]
    hb = nb // 2
    slots, size = v.tiles.shape[0], v.tiles.shape[1]
    rows = nb * size
    capf, capb = slots // n, slots // nrow
    kparts = capf // capb
    nch, ng = len(wf), len(wb)
    w, cot = v.w, v.cot
    npa = v.pa.shape[0] // n
    npc = npa // (nch - 1)
    arows = rows // npc
    npb = v.pb.shape[0] // n
    piece = rows // npb
    ppb = size // piece
    xg = [getattr(v, "x%d" % j) for j in range(nch)]
    sp, grads, abuf, bbuf, cbuf, fgs = (
        [getattr(v, "%s%d" % (name, g)) for g in range(ng)]
        for name in ("sp", "g", "a", "b", "c", "f")
    )

    def dev(d):
        return (flip(k, d) * 2 + c, q)

    def deep(dz):
        return (r, (q + dz) % n)


    def take(j):
        return pltpu.make_async_copy(
            feats.at[:, :, pl.ds(sum(wf[:j]), wf[j])], xg[j].at[pl.ds(r * nb, nb)], v.s_take.at[j]
        )

    def slot(j, d, core, h):
        return xg[j].at[pl.ds((flip(k, d) * 2 + core) * nb + h * hb, hb)]

    def same(j, d, h, to, at):
        ref = slot(j, d, c, h)
        return remote(ref, ref, v.s_same.at[j], v.r_same.at[j, at, h], dev(to))

    def own(j, d, h):
        return same(j, 0, h, d, d)

    def pass_on(j, h):
        via, to = (1, 2) if h == 0 else (2, 1)
        return same(j, via, h, to, 3)

    def inc(j, d, h):
        return same(j, d, h, d, d)

    def fwd(j, d, h):
        ref = slot(j, d, c, h)
        return remote(ref, ref, v.s_part.at[j], v.r_part.at[j], partner)

    def gather_start(j, parts=(0, 1)):
        if parts[0] == 0:
            take(j).wait()
        for i in parts:
            for d in near:
                own(j, d, (i + (d == 2)) % 2).start()
            fwd(j, 0, i).start()

    def gather_mid(j):
        for i in range(2):
            for d in near:
                h = (i + (d == 2)) % 2
                inc(j, d, h).wait_recv()
                if relay and i == 0:
                    pass_on(j, h).start()
                fwd(j, d, h).start()

    def whole(j, count):
        ref = xg[j].at[pl.ds(0, count * nb)]
        return remote(ref, ref, v.s_part.at[j], v.r_part.at[j], partner)

    def gather_end(j):
        if relay:
            for h in range(2):
                inc(j, 3, h).wait_recv()
                fwd(j, 3, h).start()
        whole(j, chips).wait_recv()

    def gather_sent(j):
        ref = xg[j].at[pl.ds(0, (chips - 1) * nb)]
        remote(ref, ref, v.s_same.at[j], v.r_same.at[j, 0, 0], partner).wait_send()
        whole(j, chips).wait_send()


    def build(o, base, cap, back):
        for s in range(cap):
            at = o * cap + s
            mat = v.tiles[lists[base * slots + at]]
            place = lists[(base + 1) * slots + at]
            if back:
                mat = jnp.transpose(mat)
            for b in range(nb):
                val = jnp.where(place == b, mat, jnp.zeros_like(mat))
                if back:
                    v.dense[o, b * size : (b + 1) * size, s * size : (s + 1) * size] = val
                else:
                    u = s % capb
                    v.dense[
                        o * kparts + s // capb, b * size : (b + 1) * size, u * size : (u + 1) * size
                    ] = val

    def forward(j):
        @pl.loop(0, n)
        def _(o):
            total = None
            for e in range(kparts):
                ids = [lists[2 * slots + o * capf + e * capb + s] for s in range(capb)]
                rhs = jnp.concatenate([xg[j][i] for i in ids], axis=0)
                res = jnp.dot(v.dense[o * kparts + e], rhs, preferred_element_type=F32)
                total = res if total is None else total + res
            total = total.astype(BF)
            if j < nch - 1:
                v.pa[pl.ds(o * npa + j * npc, npc)] = total.reshape(npc, arows, wf[j])
            else:
                v.pb[pl.ds(o * npb, npb)] = total.reshape(npb, piece, wf[j])

    def backward(g, o):
        ids = [lists[5 * slots + o * capb + s] for s in range(capb)]
        rhs = jnp.concatenate([sp[g][i] for i in ids], axis=0)
        grads[g][o] = jnp.dot(v.dense[o], rhs, preferred_element_type=F32).astype(BF)


    def chain(part, acc, count, send, recv, to, shift, d, j, first):
        at = (d + shift) * count + j
        src = part.at[d * count + j] if first else acc.at[at]
        return remote(src, acc.at[at], send.at[shift, d], recv.at[d + shift, j], to)

    def group(part, acc, count, send, recv):
        def cp_r(d, j, first=False):
            return chain(part, acc, count, send, recv, right, 1, d, j, first)

        def cp_l(d, j, first=False):
            return chain(part, acc, count, send, recv, left, 0, d, j, first)

        def hop(cp, shift, start, d, j):
            @pl.when(start)
            def _():
                cp(d, j, True).start()

            @pl.when(jnp.logical_not(start))
            def _():
                cp(d, j).wait_recv()
                at = (d + shift) * count + j
                acc[at] = (acc[at].astype(F32) + part[d * count + j].astype(F32)).astype(BF)
                cp(d, j).start()

        def live(j):
            return jnp.logical_and(j >= 0, j < count)

        def reduce_step(t):
            jr, jl = t - HOP * q, t - HOP * (last - q)

            @pl.when(live(jr))
            def _():
                @pl.loop(0, last - q)
                def _(i):
                    hop(cp_r, 1, q == 0, last - i, jr)

            @pl.when(live(jl))
            def _():
                @pl.loop(0, q)
                def _(i):
                    hop(cp_l, 0, q == last, i, jl)

        def total(j, buf):
            buf[...] = part[q * count + j].astype(F32)

            @pl.when(q > 0)
            def _():
                cp_r(q, j).wait_recv()
                buf[...] += acc[(q + 1) * count + j].astype(F32)

            @pl.when(q < last)
            def _():
                cp_l(q, j).wait_recv()
                buf[...] += acc[q * count + j].astype(F32)

        def sent():
            for d in range(n):
                ref = part.at[pl.ds(d * count, count)]

                @pl.when(q < d)
                def _():
                    remote(ref, ref, send.at[1, d], recv.at[0, 0], right).wait_send()

                @pl.when(q > d)
                def _():
                    remote(ref, ref, send.at[0, d], recv.at[0, 0], left).wait_send()

        return types.SimpleNamespace(live=live, reduce_step=reduce_step, total=total, sent=sent)

    ga = group(v.pa, v.acca, npa, v.s_ra, v.r_ra)
    gb = group(v.pb, v.accb, npb, v.s_rb, v.r_rb)


    def part_of(d, j):
        at = d * npb + j
        return at // ppb, pl.ds(pl.multiple_of((at % ppb) * piece, piece), piece)

    def cp_g(side, to, d, j):
        b, at = part_of(d, j)
        ref = sp[0].at[b, at]
        return remote(ref, ref, v.s_g.at[side, d], v.r_g.at[d, j], to)

    cp_gr = functools.partial(cp_g, 1, right)
    cp_gl = functools.partial(cp_g, 0, left)

    def cp_h(g, side, to, d, h):
        ref = sp[g].at[pl.ds(d * nb + h * hb, hb)]
        return remote(ref, ref, v.s_h.at[g, side, d], v.r_h.at[g, d, h], to)

    def cp_hr(g):
        return functools.partial(cp_h, g, 1, right)

    def cp_hl(g):
        return functools.partial(cp_h, g, 0, left)

    def send_both(cr, cl, d, j):
        @pl.when(q < last)
        def _():
            cr(d, j).start()

        @pl.when(q > 0)
        def _():
            cl(d, j).start()

    def relay_on(cr, cl, ok, j, o):
        @pl.when(jnp.logical_and(ok, q >= o))
        def _():
            cr(q - o, j).wait_recv()

            @pl.when(q < last)
            def _():
                cr(q - o, j).start()

        @pl.when(jnp.logical_and(ok, q + o <= last))
        def _():
            cl(q + o, j).wait_recv()

            @pl.when(q > 0)
            def _():
                cl(q + o, j).start()

    def own_rest(g):
        for h in range(2):
            send_both(cp_hr(g), cp_hl(g), q, h)

    def relay_rest(g, o):
        for i in range(o, n if o == 3 else min(o + 1, n)):
            for h in range(2):
                relay_on(cp_hr(g), cp_hl(g), True, h, i)

    def sent_on(g):
        send = v.s_g if g == 0 else v.s_h.at[g]
        recv = v.r_g.at[0, 0]
        for d in range(n):
            ref = sp[g].at[pl.ds(d * nb, nb)]

            @pl.when(jnp.logical_and(q >= d, q < last))
            def _():
                remote(ref, ref, send.at[1, d], recv, right).wait_send()

            @pl.when(jnp.logical_and(q <= d, q > 0))
            def _():
                remote(ref, ref, send.at[0, d], recv, left).wait_send()

    def finish_a(j):
        ga.total(j, v.fa)
        e, i = j // npc, j % npc
        v.agg[i * arows : (i + 1) * arows, e * wf[0] : (e + 1) * wf[0]] = v.fa[...].astype(BF)

    def finish(j):
        gb.total(j, v.fb)
        at = pl.ds(pl.multiple_of(j * piece, piece), piece)
        v.agg[at, sum(wf[:-1]) :] = v.fb[...].astype(BF)
        pre = jnp.dot(v.agg[at, :], w[...], preferred_element_type=F32) + bias[...]
        sig = jax.nn.sigmoid(pre)
        v.out[at, :] = (pre * sig).astype(BF)
        grad = (cot[at, :].astype(F32) * sig * (1.0 + pre * (1.0 - sig))).astype(BF)
        v.gp[at, :] = grad
        res = lax.dot_general(
            grad, w[...], (((1,), (1,)), ((), ())), preferred_element_type=F32
        ).astype(BF)
        b, sub = part_of(q, j)
        for g in range(ng):
            sp[g][b, sub, :] = res[:, sum(wb[:g]) : sum(wb[: g + 1])]
        send_both(cp_gr, cp_gl, q, j)


    cp_w1 = remote(v.wp.at[1 - c], v.w1, v.s_w.at[0], v.r_w.at[0], partner)
    w4 = v.w4

    def cp_w2(d):
        return remote(v.w1.at[flip(k, d)], v.w2.at[d - 1], v.s_w.at[1], v.r_w.at[1], dev(d))

    def cp_w3(dz):
        return remote(v.ws, v.w3.at[dz - 1], v.s_w.at[2], v.r_w.at[2], deep(dz))

    def cp_w4(d):
        return remote(w4.at[c, k], w4.at[c, k], v.s_w.at[3], v.r_w.at[3], dev(d))

    cp_w5 = remote(w4.at[c], w4.at[c], v.s_w.at[4], v.r_w.at[4], partner)

    def all_w(ref, i):
        return remote(ref, ref, v.s_w.at[i], v.r_w.at[i], partner)

    all_w2 = all_w(v.w2, 1)
    all_w3 = all_w(v.w3, 2)
    all_w4 = all_w(w4.at[0, pl.ds(0, chips - 1)], 3)

    def weight_0():
        weight_block(chips, scale, v.agg, v.gp, v.wp)
        cp_w1.start()

    def weight_1():
        cp_w1.wait_recv()
        for z in range(chips):
            v.w1[z] = (v.w1[z].astype(F32) + v.wp[c, z].astype(F32)).astype(BF)
        for d in range(1, chips):
            cp_w2(d).start()

    def weight_2():
        all_w2.wait_recv()
        total = v.w1[k].astype(F32)
        for d in range(1, chips):
            total = total + v.w2[d - 1].astype(F32)
        v.ws[...] = total.astype(BF)
        for dz in range(1, n):
            cp_w3(dz).start()

    def weight_3():
        all_w3.wait_recv()
        total = None
        for i in range(n):
            other = v.w3[jnp.maximum((q - i + n) % n - 1, 0)].astype(F32)
            term = jnp.where(q == i, v.ws[...].astype(F32), other)
            total = term if total is None else total + term
        w4[c, k] = total.astype(BF)
        for d in range(1, chips):
            cp_w4(d).start()

    def weight_4():
        all_w4.wait_recv()
        cp_w5.start()

    store_w = pltpu.make_async_copy(w4, wg, v.s_load.at[1])

    def weight_5():
        remote(
            w4.at[1 - c], w4.at[1 - c], v.s_w.at[4], v.r_w.at[4], partner
        ).wait_recv()
        bg[...] = w4[0, 0, w4.shape[2] - PAD :, :].astype(F32)[:1]
        store_w.start()

    def weight_sent():
        cp_w1.wait_send()
        for a in (all_w2, all_w3, all_w4, cp_w5):
            a.wait_send()
        store_w.wait()


    half = rows // 2

    def mine(g, d):
        return grads[g].at[flip(k, d) * 2 + c]

    def cp_a(g, d):
        return remote(
            grads[g].at[flip(k, d) * 2 + 1 - c],
            abuf[g].at[d],
            v.s_a.at[g],
            v.r_a.at[g, d],
            partner,
        )

    def cp_b(g, d, h):
        at = pl.ds(h * half, half)
        i = near.index(d)
        return remote(abuf[g].at[d, at], bbuf[g].at[i, at], v.s_b.at[g], v.r_b.at[g], dev(d))

    def all_b(g):
        return remote(bbuf[g], bbuf[g], v.s_b.at[g], v.r_b.at[g], partner)

    def cp_c(g, h):
        return remote(
            abuf[g].at[3, pl.ds(h * half, half)],
            cbuf[g].at[h],
            v.s_c.at[g],
            v.r_c.at[g, h],
            dev(h + 1),
        )

    def join(g, d):
        cp_a(g, d).wait_recv()
        add_rows(abuf[g].at[d], [abuf[g].at[d], mine(g, d)], 0, rows)

    def pass_first(g, d):
        join(g, d)
        if not relay:
            for h in range(2):
                cp_b(g, d, h).start()
        elif d == 3:
            for h in range(2):
                cp_c(g, h).start()
        else:
            cp_b(g, d, d - 1).start()

    def products(g, part):
        for i in range(part * chips // PARTS, (part + 1) * chips // PARTS):
            d = chips - 1 - i
            at = flip(k, d) * 2
            backward(g, at + 1 - c)
            cp_a(g, d).start()
            backward(g, at + c)
            if i > 0:
                pass_first(g, d + 1)

    def rows_2(g):
        if relay:
            cp_c(g, 0).wait_recv()
            add_rows(abuf[g].at[2], [abuf[g].at[2], cbuf[g].at[0]], 0, half)
            cp_b(g, 2, 0).start()
            cp_c(g, 1).wait_recv()
            at = pl.ds(half, half)
            add_rows(abuf[g].at[1, at], [abuf[g].at[1, at], cbuf[g].at[1]], 0, half)
            cp_b(g, 1, 1).start()
        join(g, 0)

    def store(g):
        return pltpu.make_async_copy(
            fgs[g], fg.at[:, pl.ds(sum(wb[:g]), wb[g])], v.s_store.at[g]
        )

    def rows_3(g):
        all_b(g).wait_recv()
        add_rows(fgs[g], [abuf[g].at[0]] + [bbuf[g].at[i] for i in range(len(near))], 0, rows)
        store(g).start()

    def rows_sent(g):
        remote(
            grads[g].at[pl.ds(0, chips)], abuf[g], v.s_a.at[g], v.r_a.at[g, 0], partner
        ).wait_send()
        all_b(g).wait_send()
        if relay:
            remote(cbuf[g], cbuf[g], v.s_c.at[g], v.r_c.at[g, 0], partner).wait_send()
        store(g).wait()


    barrier = pltpu.get_barrier_semaphore()
    peers = [partner] + [dev(d) for d in range(1, chips)] + [deep(dz) for dz in range(1, n)]
    for peer in peers:
        pl.semaphore_signal(barrier, inc=1, device_id=peer, device_id_type=MESH)
    loads = [
        pltpu.make_async_copy(a, b, v.s_load.at[i])
        for i, (a, b) in enumerate([(tiles_in, v.tiles), (w_in, w), (cot_in, cot)])
    ]
    store_out = pltpu.make_async_copy(v.out, out, v.s_load.at[0])
    for j in range(nch):
        take(j).start()
    for load in loads:
        load.start()
    pl.semaphore_wait(barrier, len(peers))

    gather_start(0)
    for load in loads:
        load.wait()

    @pl.loop(0, n)
    def _(o):
        build(o, 0, capf, False)

    gather_mid(0)
    gather_start(1)
    gather_start(2, (0,))
    gather_end(0)
    forward(0)
    ga.reduce_step(0)
    gather_mid(1)
    gather_start(2, (1,))
    ga.reduce_step(1)
    gather_end(1)
    forward(1)
    ga.reduce_step(2)
    gather_mid(2)
    ga.reduce_step(3)
    gather_end(2)
    forward(2)

    begin = 4
    wait = HOP * last
    done = npa + npb + wait - 1

    @pl.loop(begin, npa + npb + wait + RING * last)
    def _(t):
        ga.reduce_step(t)
        gb.reduce_step(t - npa)

        for e in range(npa):
            @pl.when(t == max(begin, wait + e))
            def _():
                finish_a(e)

        j = t - npa - wait

        @pl.when(gb.live(j))
        def _():
            finish(j)

        for o in range(1, n):
            p = j - RING * o
            relay_on(cp_gr, cp_gl, gb.live(p), p, o)

        o = t - begin

        @pl.when(jnp.logical_and(o >= 0, o < nrow))
        def _():
            build(o, 3, capb, True)

        @pl.when(t == done)
        def _():
            own_rest(1)
            weight_0()
            weight_1()
            store_out.start()

    relay_rest(1, 1)
    products(0, 0)
    own_rest(2)
    products(0, 1)
    products(0, 2)
    products(0, 3)
    relay_rest(1, 2)
    relay_rest(1, 3)
    weight_2()
    rows_2(0)
    relay_rest(2, 1)
    products(1, 0)
    products(1, 1)
    products(1, 2)
    products(1, 3)
    rows_3(0)
    rows_2(1)
    relay_rest(2, 2)
    weight_3()
    relay_rest(2, 3)
    products(2, 0)
    products(2, 1)
    products(2, 2)
    products(2, 3)
    rows_3(1)
    rows_2(2)
    weight_4()
    weight_5()
    rows_3(2)

    for j in range(nch):
        gather_sent(j)
    ga.sent()
    gb.sent()
    for g in range(ng):
        sent_on(g)
    for g in range(ng):
        rows_sent(g)
    weight_sent()
    store_out.wait()


def tail_kernel(out_in, fg_in, parts, bg_in, out, fg, wg, bg):
    out[...] = out_in[...]
    fg[...] = fg_in[...]
    count = parts.shape[1]
    rows = wg.shape[0] // (2 * count)
    for a in range(2):
        for b in range(count):
            at = (a * count + b) * rows
            wg[at : at + rows, :] = parts[a, b, :rows, :].astype(F32)
    bg[...] = bg_in[...]


VM = pl.BlockSpec(memory_space=pltpu.VMEM)
SM = pl.BlockSpec(memory_space=pltpu.SMEM)
ANY = pl.BlockSpec(memory_space=pl.ANY)


def dma(*shape):
    return pltpu.SemaphoreType.DMA(shape)


def on_device(features, weight, bias, cotangent, tile_values, tile_rows, tile_cols, tile_counts):
    nrow = lax.axis_size("row")
    ncol = lax.axis_size("col")
    node_dev, width = features.shape
    slots, size = tile_values.shape[2], tile_values.shape[3]
    nb = node_dev // size
    chips = nrow // 2
    scale = 1.0 / math.sqrt(node_dev * nrow * ncol)
    values = tile_values.reshape(slots, size, size)

    lists = pl.pallas_call(
        functools.partial(list_kernel, nrow, ncol, nb),
        out_shape=jax.ShapeDtypeStruct((LISTS * slots,), jnp.int32),
        in_specs=[SM, SM, SM],
        out_specs=SM,
        scratch_shapes=[pltpu.SMEM((nrow + ncol,), jnp.int32)],
        name="lists",
    )(tile_counts.reshape(1), tile_rows.reshape(slots), tile_cols.reshape(slots))

    wf = (width // 4, width // 4, width - 2 * (width // 4))
    wb = (width // 2, width // 4, width - width // 2 - width // 4)
    nch, ng = len(wf), len(wb)
    npa = 4
    arows = node_dev * (nch - 1) // npa
    piece = size // 2
    npb = node_dev // piece
    pr = width // (2 * chips) + PAD
    capb = slots // nrow

    def vm(*shape, dtype=BF):
        return pltpu.VMEM(shape, dtype)

    scratch = {"x%d" % j: vm(nrow * nb, size, wf[j]) for j in range(nch)}
    scratch.update(
        tiles=vm(slots, size, size),
        dense=vm(nrow, node_dev, capb * size),
        pa=vm(ncol * npa, arows, wf[0]),
        pb=vm(ncol * npb, piece, wf[-1]),
        acca=vm((ncol + 1) * npa, arows, wf[0]),
        accb=vm((ncol + 1) * npb, piece, wf[-1]),
        fa=vm(arows, wf[0], dtype=F32),
        fb=vm(piece, wf[-1], dtype=F32),
        w=vm(width, width),
        cot=vm(node_dev, width),
        agg=vm(node_dev, width),
        gp=vm(node_dev, width),
        wp=vm(2, chips, pr, width),
        w1=vm(chips, pr, width),
        w2=vm(chips - 1, pr, width),
        w3=vm(ncol - 1, pr, width),
        w4=vm(2, chips, pr, width),
        out=vm(node_dev, width),
        ws=vm(pr, width),
        s_take=dma(nch),
        s_load=dma(3),
        s_same=dma(nch),
        r_same=dma(nch, chips, 2),
        s_part=dma(nch),
        r_part=dma(nch),
        s_ra=dma(2, ncol),
        r_ra=dma(ncol + 1, npa),
        s_rb=dma(2, ncol),
        r_rb=dma(ncol + 1, npb),
        s_g=dma(2, ncol),
        r_g=dma(ncol, npb),
        s_h=dma(ng, 2, ncol),
        r_h=dma(ng, ncol, 2),
        s_a=dma(ng),
        r_a=dma(ng, chips),
        s_b=dma(ng),
        r_b=dma(ng),
        s_c=dma(ng),
        r_c=dma(ng, 2),
        s_w=dma(5),
        r_w=dma(5),
        s_store=dma(ng),
    )
    others = chips - 1 - (chips == 4)
    for g in range(ng):
        scratch["sp%d" % g] = vm(ncol * nb, size, wb[g])
        scratch["g%d" % g] = vm(nrow, node_dev, wb[g])
        scratch["a%d" % g] = vm(chips, node_dev, wb[g])
        scratch["b%d" % g] = vm(others, node_dev, wb[g])
        scratch["c%d" % g] = vm(2, node_dev // 2, wb[g])
        scratch["f%d" % g] = vm(node_dev, wb[g])

    out, fg, parts, bg = pl.pallas_call(
        functools.partial(mega_kernel, tuple(scratch), ncol, nrow, nb, scale, wf, wb),
        out_shape=[
            jax.ShapeDtypeStruct((node_dev, width), BF),
            jax.ShapeDtypeStruct((node_dev, width), BF),
            jax.ShapeDtypeStruct((2, chips, pr, width), BF),
            jax.ShapeDtypeStruct((1, width), F32),
        ],
        in_specs=[SM, ANY, ANY, ANY, VM, ANY],
        out_specs=[ANY, ANY, ANY, VM],
        scratch_shapes=list(scratch.values()),
        compiler_params=pltpu.CompilerParams(
            collective_id=0, has_side_effects=True, vmem_limit_bytes=60 << 20
        ),
        name="layer",
    )(
        lists,
        features.reshape(nb, size, width),
        values,
        weight,
        bias.reshape(1, width),
        cotangent,
    )

    out, fg, wg, bg = pl.pallas_call(
        tail_kernel,
        out_shape=[
            jax.ShapeDtypeStruct((node_dev, width), BF),
            jax.ShapeDtypeStruct((node_dev, width), BF),
            jax.ShapeDtypeStruct((width, width), F32),
            jax.ShapeDtypeStruct((1, width), F32),
        ],
        in_specs=[VM] * 4,
        out_specs=[VM] * 4,
        name="tail",
    )(out, fg, parts, bg)
    return (out, fg, wg, bg.reshape(width))


def solution(mesh):
    return jax.shard_map(
        on_device,
        mesh=mesh,
        in_specs=(
            P(("row", "col"), None),
            P(),
            P(),
            P(("row", "col"), None),
            P("row", "col", None, None, None),
            P("row", "col", None),
            P("row", "col", None),
            P("row", "col"),
        ),
        out_specs=(P(("row", "col"), None), P(("row", "col"), None), P(), P()),
        check_vma=False,
    )
```

```python
import functools
import math
import types

import jax
import jax.numpy as jnp
from jax import lax
from jax.experimental import pallas as pl
from jax.experimental.pallas import tpu as pltpu
from jax.sharding import PartitionSpec as P

MESH = pl.DeviceIdType.MESH
BF = jnp.bfloat16
F32 = jnp.float32
PAD = 16
PARTS = 4
HOP = 1
RING = 1
LISTS = 6


def flip(k, d):
    out = 0
    for b in range(8):
        step = 1 << b
        if isinstance(d, int):
            if d < step:
                bit = 0
            else:
                bit = (d // step) % 2
        else:
            bit = (d // step) % 2
        kb = (k // step) % 2
        if isinstance(bit, int):
            out = out + step * ((1 - kb) if bit else kb)
        else:
            out = out + step * (kb + bit - 2 * kb * bit)
    return out


def remote(src, dst, send, recv, to):
    return pltpu.make_async_remote_copy(
        src_ref=src, dst_ref=dst, send_sem=send, recv_sem=recv, device_id=to, device_id_type=MESH
    )


def list_kernel(nrow, ncol, blk, counts, rows, cols, out, lens):
    slots = rows.shape[0]
    capf, capb = slots // ncol, slots // nrow
    span = blk * ncol

    @pl.loop(0, slots, unroll=8)
    def _(i):
        out[i] = 0
        out[slots + i] = -1
        out[2 * slots + i] = 0
        out[3 * slots + i] = 0
        out[4 * slots + i] = -1
        out[5 * slots + i] = 0

    @pl.loop(0, nrow + ncol)
    def _(i):
        lens[i] = 0

    @pl.loop(0, counts[0, 0])
    def _(k):
        row = rows[k] % span
        col = cols[k]
        o = row // blk
        at = o * capf + lens[o]
        lens[o] = lens[o] + 1
        dev = col // span
        src = dev * blk + col % blk
        out[at] = k
        out[slots + at] = row % blk
        out[2 * slots + at] = src
        bt = dev * capb + lens[ncol + dev]
        lens[ncol + dev] = lens[ncol + dev] + 1
        out[3 * slots + bt] = k
        out[4 * slots + bt] = col % blk
        out[5 * slots + bt] = row


def add_rows(dst, srcs, begin, count):
    step = 64

    @pl.loop(0, count // step)
    def _(i):
        at = pl.ds(pl.multiple_of(begin + i * step, step), step)
        total = srcs[0][at, :].astype(F32)
        for s in srcs[1:]:
            total = total + s[at, :].astype(F32)
        dst[at, :] = total.astype(dst.dtype)


def weight_block(parts, scale, agg, gp, wp):
    width = agg.shape[1]
    rows = width // (2 * parts)
    total = jnp.sum(gp[...].astype(F32), axis=0, keepdims=True) * scale
    pad = jnp.broadcast_to(total, (PAD, width)).astype(BF)
    step = 128
    for t in range(width // step):
        res = lax.dot_general(
            agg[:, t * step : (t + 1) * step],
            gp[...],
            (((0,), (0,)), ((), ())),
            preferred_element_type=F32,
        )
        res = (res * scale).astype(BF)
        for u in range(step // rows):
            p = (t * step) // rows + u
            wp[p // parts, p % parts, :rows, :] = res[u * rows : (u + 1) * rows]
            wp[p // parts, p % parts, rows:, :] = pad


def mega_kernel(
    names, n, nrow, nb, scale, wf, wb, lists, feats, tiles_in, w_in, bias, cot_in, out, fg, wg, bg,
    *scratch
):
    v = types.SimpleNamespace(**dict(zip(names, scratch)))
    r, q = lax.axis_index("row"), lax.axis_index("col")
    k, c = r // 2, r % 2
    chips = nrow // 2
    last = n - 1
    right, left = (r, jnp.minimum(q + 1, last)), (r, jnp.maximum(q - 1, 0))
    partner = (k * 2 + 1 - c, q)
    relay = chips == 4
    near = [d for d in range(1, chips) if not (relay and d == 3)]
    hb = nb // 2
    slots, size = v.tiles.shape[0], v.tiles.shape[1]
    rows = nb * size
    capf, capb = slots // n, slots // nrow
    kparts = capf // capb
    nch, ng = len(wf), len(wb)
    w, cot = v.w, v.cot
    npa = v.pa.shape[0] // n
    npc = npa // (nch - 1)
    arows = rows // npc
    npb = v.pb.shape[0] // n
    piece = rows // npb
    ppb = size // piece
    xg = [getattr(v, "x%d" % j) for j in range(nch)]
    sp, grads, abuf, bbuf, cbuf, fgs = (
        [getattr(v, "%s%d" % (name, g)) for g in range(ng)]
        for name in ("sp", "g", "a", "b", "c", "f")
    )

    def dev(d):
        return (flip(k, d) * 2 + c, q)

    def deep(dz):
        return (r, (q + dz) % n)


    def take(j):
        return pltpu.make_async_copy(
            feats.at[:, :, pl.ds(sum(wf[:j]), wf[j])], xg[j].at[pl.ds(r * nb, nb)], v.s_take.at[j]
        )

    def slot(j, d, core, h):
        return xg[j].at[pl.ds((flip(k, d) * 2 + core) * nb + h * hb, hb)]

    def same(j, d, h, to, at):
        ref = slot(j, d, c, h)
        return remote(ref, ref, v.s_same.at[j], v.r_same.at[j, at, h], dev(to))

    def own(j, d, h):
        return same(j, 0, h, d, d)

    def pass_on(j, h):
        via, to = (1, 2) if h == 0 else (2, 1)
        return same(j, via, h, to, 3)

    def inc(j, d, h):
        return same(j, d, h, d, d)

    def fwd(j, d, h):
        ref = slot(j, d, c, h)
        return remote(ref, ref, v.s_part.at[j], v.r_part.at[j], partner)

    def gather_start(j, parts=(0, 1)):
        if parts[0] == 0:
            take(j).wait()
        for i in parts:
            for d in near:
                own(j, d, (i + (d == 2)) % 2).start()
            fwd(j, 0, i).start()

    def gather_mid(j):
        for i in range(2):
            for d in near:
                h = (i + (d == 2)) % 2
                inc(j, d, h).wait_recv()
                if relay and i == 0:
                    pass_on(j, h).start()
                fwd(j, d, h).start()

    def whole(j, count):
        ref = xg[j].at[pl.ds(0, count * nb)]
        return remote(ref, ref, v.s_part.at[j], v.r_part.at[j], partner)

    def gather_end(j):
        if relay:
            for h in range(2):
                inc(j, 3, h).wait_recv()
                fwd(j, 3, h).start()
        whole(j, chips).wait_recv()

    def gather_sent(j):
        ref = xg[j].at[pl.ds(0, (chips - 1) * nb)]
        remote(ref, ref, v.s_same.at[j], v.r_same.at[j, 0, 0], partner).wait_send()
        whole(j, chips).wait_send()


    def build(o, base, cap, back):
        for s in range(cap):
            at = o * cap + s
            mat = v.tiles[lists[base * slots + at]]
            place = lists[(base + 1) * slots + at]
            if back:
                mat = jnp.transpose(mat)
            for b in range(nb):
                val = jnp.where(place == b, mat, jnp.zeros_like(mat))
                if back:
                    v.dense[o, b * size : (b + 1) * size, s * size : (s + 1) * size] = val
                else:
                    u = s % capb
                    v.dense[
                        o * kparts + s // capb, b * size : (b + 1) * size, u * size : (u + 1) * size
                    ] = val

    def forward(j):
        @pl.loop(0, n)
        def _(o):
            total = None
            for e in range(kparts):
                ids = [lists[2 * slots + o * capf + e * capb + s] for s in range(capb)]
                rhs = jnp.concatenate([xg[j][i] for i in ids], axis=0)
                res = jnp.dot(v.dense[o * kparts + e], rhs, preferred_element_type=F32)
                total = res if total is None else total + res
            total = total.astype(BF)
            if j < nch - 1:
                v.pa[pl.ds(o * npa + j * npc, npc)] = total.reshape(npc, arows, wf[j])
            else:
                v.pb[pl.ds(o * npb, npb)] = total.reshape(npb, piece, wf[j])

    def backward(g, o):
        ids = [lists[5 * slots + o * capb + s] for s in range(capb)]
        rhs = jnp.concatenate([sp[g][i] for i in ids], axis=0)
        grads[g][o] = jnp.dot(v.dense[o], rhs, preferred_element_type=F32).astype(BF)


    def chain(part, acc, count, send, recv, to, shift, d, j, first):
        at = (d + shift) * count + j
        src = part.at[d * count + j] if first else acc.at[at]
        return remote(src, acc.at[at], send.at[shift, d], recv.at[d + shift, j], to)

    def group(part, acc, count, send, recv):
        def cp_r(d, j, first=False):
            return chain(part, acc, count, send, recv, right, 1, d, j, first)

        def cp_l(d, j, first=False):
            return chain(part, acc, count, send, recv, left, 0, d, j, first)

        def hop(cp, shift, start, d, j):
            @pl.when(start)
            def _():
                cp(d, j, True).start()

            @pl.when(jnp.logical_not(start))
            def _():
                cp(d, j).wait_recv()
                at = (d + shift) * count + j
                acc[at] = (acc[at].astype(F32) + part[d * count + j].astype(F32)).astype(BF)
                cp(d, j).start()

        def live(j):
            return jnp.logical_and(j >= 0, j < count)

        def reduce_step(t):
            jr, jl = t - HOP * q, t - HOP * (last - q)

            @pl.when(live(jr))
            def _():
                @pl.loop(0, last - q)
                def _(i):
                    hop(cp_r, 1, q == 0, last - i, jr)

            @pl.when(live(jl))
            def _():
                @pl.loop(0, q)
                def _(i):
                    hop(cp_l, 0, q == last, i, jl)

        def total(j, buf):
            buf[...] = part[q * count + j].astype(F32)

            @pl.when(q > 0)
            def _():
                cp_r(q, j).wait_recv()
                buf[...] += acc[(q + 1) * count + j].astype(F32)

            @pl.when(q < last)
            def _():
                cp_l(q, j).wait_recv()
                buf[...] += acc[q * count + j].astype(F32)

        def sent():
            for d in range(n):
                ref = part.at[pl.ds(d * count, count)]

                @pl.when(q < d)
                def _():
                    remote(ref, ref, send.at[1, d], recv.at[0, 0], right).wait_send()

                @pl.when(q > d)
                def _():
                    remote(ref, ref, send.at[0, d], recv.at[0, 0], left).wait_send()

        return types.SimpleNamespace(live=live, reduce_step=reduce_step, total=total, sent=sent)

    ga = group(v.pa, v.acca, npa, v.s_ra, v.r_ra)
    gb = group(v.pb, v.accb, npb, v.s_rb, v.r_rb)


    def part_of(d, j):
        at = d * npb + j
        return at // ppb, pl.ds(pl.multiple_of((at % ppb) * piece, piece), piece)

    def cp_g(side, to, d, j):
        b, at = part_of(d, j)
        ref = sp[0].at[b, at]
        return remote(ref, ref, v.s_g.at[side, d], v.r_g.at[d, j], to)

    cp_gr = functools.partial(cp_g, 1, right)
    cp_gl = functools.partial(cp_g, 0, left)

    def cp_h(g, side, to, d, h):
        ref = sp[g].at[pl.ds(d * nb + h * hb, hb)]
        return remote(ref, ref, v.s_h.at[g - 1, side, d], v.r_h.at[g - 1, d, h], to)

    def cp_hr(g):
        return functools.partial(cp_h, g, 1, right)

    def cp_hl(g):
        return functools.partial(cp_h, g, 0, left)

    def send_both(cr, cl, d, j):
        @pl.when(q < last)
        def _():
            cr(d, j).start()

        @pl.when(q > 0)
        def _():
            cl(d, j).start()

    def relay_on(cr, cl, ok, j, o):
        @pl.when(jnp.logical_and(ok, q >= o))
        def _():
            cr(q - o, j).wait_recv()

            @pl.when(q < last)
            def _():
                cr(q - o, j).start()

        @pl.when(jnp.logical_and(ok, q + o <= last))
        def _():
            cl(q + o, j).wait_recv()

            @pl.when(q > 0)
            def _():
                cl(q + o, j).start()

    def own_rest(g):
        for h in range(2):
            send_both(cp_hr(g), cp_hl(g), q, h)

    def relay_rest(g, o):
        for i in range(o, n if o == 3 else min(o + 1, n)):
            for h in range(2):
                relay_on(cp_hr(g), cp_hl(g), True, h, i)

    def sent_on(g):
        send = v.s_g if g == 0 else v.s_h.at[g - 1]
        recv = v.r_g.at[0, 0]
        for d in range(n):
            ref = sp[g].at[pl.ds(d * nb, nb)]

            @pl.when(jnp.logical_and(q >= d, q < last))
            def _():
                remote(ref, ref, send.at[1, d], recv, right).wait_send()

            @pl.when(jnp.logical_and(q <= d, q > 0))
            def _():
                remote(ref, ref, send.at[0, d], recv, left).wait_send()

    def finish_a(j):
        ga.total(j, v.fa)
        e, i = j // npc, j % npc
        v.agg[i * arows : (i + 1) * arows, e * wf[0] : (e + 1) * wf[0]] = v.fa[...].astype(BF)

    def finish(j):
        gb.total(j, v.fb)
        at = pl.ds(pl.multiple_of(j * piece, piece), piece)
        v.agg[at, sum(wf[:-1]) :] = v.fb[...].astype(BF)
        pre = jnp.dot(v.agg[at, :], w[...], preferred_element_type=F32) + bias[...]
        sig = jax.nn.sigmoid(pre)
        v.out[at, :] = (pre * sig).astype(BF)
        grad = (cot[at, :].astype(F32) * sig * (1.0 + pre * (1.0 - sig))).astype(BF)
        v.gp[at, :] = grad
        res = lax.dot_general(
            grad, w[...], (((1,), (1,)), ((), ())), preferred_element_type=F32
        ).astype(BF)
        b, sub = part_of(q, j)
        for g in range(ng):
            sp[g][b, sub, :] = res[:, sum(wb[:g]) : sum(wb[: g + 1])]
        send_both(cp_gr, cp_gl, q, j)


    cp_w1 = remote(v.wp.at[1 - c], v.w1, v.s_w.at[0], v.r_w.at[0], partner)
    w4 = v.w4

    def cp_w2(d):
        return remote(v.w1.at[flip(k, d)], v.w2.at[d - 1], v.s_w.at[1], v.r_w.at[1], dev(d))

    def cp_w3(dz):
        return remote(v.ws, v.w3.at[dz - 1], v.s_w.at[2], v.r_w.at[2], deep(dz))

    def cp_w4(d):
        return remote(w4.at[c, k], w4.at[c, k], v.s_w.at[3], v.r_w.at[3], dev(d))

    cp_w5 = remote(w4.at[c], w4.at[c], v.s_w.at[4], v.r_w.at[4], partner)

    def all_w(ref, i):
        return remote(ref, ref, v.s_w.at[i], v.r_w.at[i], partner)

    all_w2 = all_w(v.w2, 1)
    all_w3 = all_w(v.w3, 2)
    all_w4 = all_w(w4.at[0, pl.ds(0, chips - 1)], 3)

    def weight_0():
        weight_block(chips, scale, v.agg, v.gp, v.wp)
        cp_w1.start()

    def weight_1():
        cp_w1.wait_recv()
        for z in range(chips):
            v.w1[z] = (v.w1[z].astype(F32) + v.wp[c, z].astype(F32)).astype(BF)
        for d in range(1, chips):
            cp_w2(d).start()

    def weight_2():
        all_w2.wait_recv()
        total = v.w1[k].astype(F32)
        for d in range(1, chips):
            total = total + v.w2[d - 1].astype(F32)
        v.ws[...] = total.astype(BF)
        for dz in range(1, n):
            cp_w3(dz).start()

    def weight_3():
        all_w3.wait_recv()
        total = None
        for i in range(n):
            other = v.w3[jnp.maximum((q - i + n) % n - 1, 0)].astype(F32)
            term = jnp.where(q == i, v.ws[...].astype(F32), other)
            total = term if total is None else total + term
        w4[c, k] = total.astype(BF)
        for d in range(1, chips):
            cp_w4(d).start()

    def weight_4():
        all_w4.wait_recv()
        cp_w5.start()

    store_w = pltpu.make_async_copy(w4, wg, v.s_load.at[1])

    def weight_5():
        remote(
            w4.at[1 - c], w4.at[1 - c], v.s_w.at[4], v.r_w.at[4], partner
        ).wait_recv()
        bg[...] = w4[0, 0, w4.shape[2] - PAD :, :].astype(F32)[:1]
        store_w.start()

    def weight_sent():
        cp_w1.wait_send()
        for a in (all_w2, all_w3, all_w4, cp_w5):
            a.wait_send()
        store_w.wait()


    half = rows // 2

    def mine(g, d):
        return grads[g].at[flip(k, d) * 2 + c]

    def cp_a(g, d):
        return remote(
            grads[g].at[flip(k, d) * 2 + 1 - c],
            abuf[g].at[d],
            v.s_a.at[g],
            v.r_a.at[g, d],
            partner,
        )

    def cp_b(g, d, h):
        at = pl.ds(h * half, half)
        i = near.index(d)
        return remote(abuf[g].at[d, at], bbuf[g].at[i, at], v.s_b.at[g], v.r_b.at[g], dev(d))

    def all_b(g):
        return remote(bbuf[g], bbuf[g], v.s_b.at[g], v.r_b.at[g], partner)

    def cp_c(g, h):
        return remote(
            abuf[g].at[3, pl.ds(h * half, half)],
            cbuf[g].at[h],
            v.s_c.at[g],
            v.r_c.at[g, h],
            dev(h + 1),
        )

    def join(g, d):
        cp_a(g, d).wait_recv()
        add_rows(abuf[g].at[d], [abuf[g].at[d], mine(g, d)], 0, rows)

    def pass_first(g, d):
        join(g, d)
        if not relay:
            for h in range(2):
                cp_b(g, d, h).start()
        elif d == 3:
            for h in range(2):
                cp_c(g, h).start()
        else:
            cp_b(g, d, d - 1).start()

    def products(g, part):
        for i in range(part * chips // PARTS, (part + 1) * chips // PARTS):
            d = chips - 1 - i
            at = flip(k, d) * 2
            backward(g, at + 1 - c)
            cp_a(g, d).start()
            backward(g, at + c)
            if i > 0:
                pass_first(g, d + 1)

    def rows_2(g):
        if relay:
            cp_c(g, 0).wait_recv()
            add_rows(abuf[g].at[2], [abuf[g].at[2], cbuf[g].at[0]], 0, half)
            cp_b(g, 2, 0).start()
            cp_c(g, 1).wait_recv()
            at = pl.ds(half, half)
            add_rows(abuf[g].at[1, at], [abuf[g].at[1, at], cbuf[g].at[1]], 0, half)
            cp_b(g, 1, 1).start()
        join(g, 0)

    def store(g):
        return pltpu.make_async_copy(
            fgs[g], fg.at[:, pl.ds(sum(wb[:g]), wb[g])], v.s_store.at[g]
        )

    def rows_3(g):
        all_b(g).wait_recv()
        add_rows(fgs[g], [abuf[g].at[0]] + [bbuf[g].at[i] for i in range(len(near))], 0, rows)
        store(g).start()

    def rows_sent(g):
        remote(
            grads[g].at[pl.ds(0, chips)], abuf[g], v.s_a.at[g], v.r_a.at[g, 0], partner
        ).wait_send()
        all_b(g).wait_send()
        if relay:
            remote(cbuf[g], cbuf[g], v.s_c.at[g], v.r_c.at[g, 0], partner).wait_send()
        store(g).wait()


    barrier = pltpu.get_barrier_semaphore()
    peers = [partner] + [dev(d) for d in range(1, chips)] + [deep(dz) for dz in range(1, n)]
    for peer in peers:
        pl.semaphore_signal(barrier, inc=1, device_id=peer, device_id_type=MESH)
    loads = [
        pltpu.make_async_copy(a, b, v.s_load.at[i])
        for i, (a, b) in enumerate([(tiles_in, v.tiles), (w_in, w), (cot_in, cot)])
    ]
    store_out = pltpu.make_async_copy(v.out, out, v.s_load.at[0])
    for j in range(nch):
        take(j).start()
    for load in loads:
        load.start()
    pl.semaphore_wait(barrier, len(peers))

    gather_start(0)
    for load in loads:
        load.wait()

    @pl.loop(0, n)
    def _(o):
        build(o, 0, capf, False)

    gather_mid(0)
    gather_start(1)
    gather_start(2, (0,))
    gather_end(0)
    forward(0)
    ga.reduce_step(0)
    gather_mid(1)
    gather_start(2, (1,))
    ga.reduce_step(1)
    gather_end(1)
    forward(1)
    ga.reduce_step(2)
    gather_mid(2)
    ga.reduce_step(3)
    gather_end(2)
    forward(2)

    begin = 4
    wait = HOP * last
    done = npa + npb + wait - 1

    @pl.loop(begin, npa + npb + wait + RING * last)
    def _(t):
        ga.reduce_step(t)
        gb.reduce_step(t - npa)

        for e in range(npa):
            @pl.when(t == max(begin, wait + e))
            def _():
                finish_a(e)

        j = t - npa - wait

        @pl.when(gb.live(j))
        def _():
            finish(j)

        for o in range(1, n):
            p = j - RING * o
            relay_on(cp_gr, cp_gl, gb.live(p), p, o)

        o = t - begin

        @pl.when(jnp.logical_and(o >= 0, o < nrow))
        def _():
            build(o, 3, capb, True)

        @pl.when(t == done)
        def _():
            own_rest(1)
            weight_0()
            weight_1()
            store_out.start()

    relay_rest(1, 1)
    products(0, 0)
    own_rest(2)
    products(0, 1)
    products(0, 2)
    products(0, 3)
    relay_rest(1, 2)
    relay_rest(1, 3)
    weight_2()
    rows_2(0)
    relay_rest(2, 1)
    products(1, 0)
    products(1, 1)
    products(1, 2)
    products(1, 3)
    rows_3(0)
    rows_2(1)
    relay_rest(2, 2)
    weight_3()
    relay_rest(2, 3)
    products(2, 0)
    products(2, 1)
    products(2, 2)
    products(2, 3)
    rows_3(1)
    for j in range(nch):
        gather_sent(j)
    ga.sent()
    gb.sent()
    rows_2(2)
    weight_4()
    weight_5()
    for g in range(ng):
        sent_on(g)
    for g in range(ng - 1):
        rows_sent(g)
    rows_3(2)

    rows_sent(ng - 1)
    weight_sent()
    store_out.wait()


def tail_kernel(out_in, fg_in, parts, bg_in, out, fg, wg, bg):
    out[...] = out_in[...]
    fg[...] = fg_in[...]
    count = parts.shape[1]
    rows = wg.shape[0] // (2 * count)
    for a in range(2):
        for b in range(count):
            at = (a * count + b) * rows
            wg[at : at + rows, :] = parts[a, b, :rows, :].astype(F32)
    bg[...] = bg_in[...]


VM = pl.BlockSpec(memory_space=pltpu.VMEM)
SM = pl.BlockSpec(memory_space=pltpu.SMEM)
ANY = pl.BlockSpec(memory_space=pl.ANY)


def dma(*shape):
    return pltpu.SemaphoreType.DMA(shape)


def on_device(features, weight, bias, cotangent, tile_values, tile_rows, tile_cols, tile_counts):
    nrow = lax.axis_size("row")
    ncol = lax.axis_size("col")
    node_dev, width = features.shape
    slots, size = tile_values.shape[2], tile_values.shape[3]
    nb = node_dev // size
    chips = nrow // 2
    scale = 1.0 / math.sqrt(node_dev * nrow * ncol)
    values = tile_values.reshape(slots, size, size)

    lists = pl.pallas_call(
        functools.partial(list_kernel, nrow, ncol, nb),
        out_shape=jax.ShapeDtypeStruct((LISTS * slots,), jnp.int32),
        in_specs=[SM, SM, SM],
        out_specs=SM,
        scratch_shapes=[pltpu.SMEM((nrow + ncol,), jnp.int32)],
        name="lists",
    )(tile_counts, tile_rows.reshape(slots), tile_cols.reshape(slots))

    wf = (width // 4, width // 4, width - 2 * (width // 4))
    wb = (width // 2, width // 4, width - width // 2 - width // 4)
    nch, ng = len(wf), len(wb)
    npa = 4
    arows = node_dev * (nch - 1) // npa
    piece = size // 2
    npb = node_dev // piece
    pr = width // (2 * chips) + PAD
    capb = slots // nrow

    def vm(*shape, dtype=BF):
        return pltpu.VMEM(shape, dtype)

    scratch = {"x%d" % j: vm(nrow * nb, size, wf[j]) for j in range(nch)}
    scratch.update(
        tiles=vm(slots, size, size),
        dense=vm(nrow, node_dev, capb * size),
        pa=vm(ncol * npa, arows, wf[0]),
        pb=vm(ncol * npb, piece, wf[-1]),
        acca=vm((ncol + 1) * npa, arows, wf[0]),
        accb=vm((ncol + 1) * npb, piece, wf[-1]),
        fa=vm(arows, wf[0], dtype=F32),
        fb=vm(piece, wf[-1], dtype=F32),
        w=vm(width, width),
        cot=vm(node_dev, width),
        agg=vm(node_dev, width),
        gp=vm(node_dev, width),
        wp=vm(2, chips, pr, width),
        w1=vm(chips, pr, width),
        w2=vm(chips - 1, pr, width),
        w3=vm(ncol - 1, pr, width),
        w4=vm(2, chips, pr, width),
        out=vm(node_dev, width),
        ws=vm(pr, width),
        s_take=dma(nch),
        s_load=dma(3),
        s_same=dma(nch),
        r_same=dma(nch, chips, 2),
        s_part=dma(nch),
        r_part=dma(nch),
        s_ra=dma(2, ncol),
        r_ra=dma(ncol + 1, npa),
        s_rb=dma(2, ncol),
        r_rb=dma(ncol + 1, npb),
        s_g=dma(2, ncol),
        r_g=dma(ncol, npb),
        s_h=dma(ng - 1, 2, ncol),
        r_h=dma(ng - 1, ncol, 2),
        s_a=dma(ng),
        r_a=dma(ng, chips),
        s_b=dma(ng),
        r_b=dma(ng),
        s_c=dma(ng),
        r_c=dma(ng, 2),
        s_w=dma(5),
        r_w=dma(5),
        s_store=dma(ng),
    )
    others = chips - 1 - (chips == 4)
    for g in range(ng):
        scratch["sp%d" % g] = vm(ncol * nb, size, wb[g])
        scratch["g%d" % g] = vm(nrow, node_dev, wb[g])
        scratch["a%d" % g] = vm(chips, node_dev, wb[g])
        scratch["b%d" % g] = vm(others, node_dev, wb[g])
        scratch["c%d" % g] = vm(2, node_dev // 2, wb[g])
        scratch["f%d" % g] = vm(node_dev, wb[g])

    out, fg, parts, bg = pl.pallas_call(
        functools.partial(mega_kernel, tuple(scratch), ncol, nrow, nb, scale, wf, wb),
        out_shape=[
            jax.ShapeDtypeStruct((node_dev, width), BF),
            jax.ShapeDtypeStruct((node_dev, width), BF),
            jax.ShapeDtypeStruct((2, chips, pr, width), BF),
            jax.ShapeDtypeStruct((1, width), F32),
        ],
        in_specs=[SM, ANY, ANY, ANY, VM, ANY],
        out_specs=[ANY, ANY, ANY, VM],
        scratch_shapes=list(scratch.values()),
        compiler_params=pltpu.CompilerParams(
            collective_id=0, has_side_effects=True, vmem_limit_bytes=60 << 20
        ),
        name="layer",
    )(
        lists,
        features.reshape(nb, size, width),
        values,
        weight,
        bias.reshape(1, width),
        cotangent,
    )

    out, fg, wg, bg = pl.pallas_call(
        tail_kernel,
        out_shape=[
            jax.ShapeDtypeStruct((node_dev, width), BF),
            jax.ShapeDtypeStruct((node_dev, width), BF),
            jax.ShapeDtypeStruct((width, width), F32),
            jax.ShapeDtypeStruct((1, width), F32),
        ],
        in_specs=[VM] * 4,
        out_specs=[VM] * 4,
        name="tail",
    )(out, fg, parts, bg)
    return (out, fg, wg, bg.reshape(width))


def solution(mesh):
    return jax.shard_map(
        on_device,
        mesh=mesh,
        in_specs=(
            P(("row", "col"), None),
            P(),
            P(),
            P(("row", "col"), None),
            P("row", "col", None, None, None),
            P("row", "col", None),
            P("row", "col", None),
            P("row", "col"),
        ),
        out_specs=(P(("row", "col"), None), P(("row", "col"), None), P(), P()),
        check_vma=False,
    )
```

```python
import functools
import math
import types

import jax
import jax.numpy as jnp
from jax import lax
from jax.experimental import pallas as pl
from jax.experimental.pallas import tpu as pltpu
from jax.sharding import PartitionSpec as P

MESH = pl.DeviceIdType.MESH
BF = jnp.bfloat16
F32 = jnp.float32
PAD = 16
PARTS = 4
HOP = 1
RING = 1
LISTS = 6


def flip(k, d):
    out = 0
    for b in range(8):
        step = 1 << b
        if isinstance(d, int):
            if d < step:
                bit = 0
            else:
                bit = (d // step) % 2
        else:
            bit = (d // step) % 2
        kb = (k // step) % 2
        if isinstance(bit, int):
            out = out + step * ((1 - kb) if bit else kb)
        else:
            out = out + step * (kb + bit - 2 * kb * bit)
    return out


def remote(src, dst, send, recv, to):
    return pltpu.make_async_remote_copy(
        src_ref=src, dst_ref=dst, send_sem=send, recv_sem=recv, device_id=to, device_id_type=MESH
    )


def list_kernel(nrow, ncol, blk, counts, rows, cols, out, lens):
    slots = rows.shape[0]
    capf, capb = slots // ncol, slots // nrow
    span = blk * ncol

    @pl.loop(0, slots, unroll=8)
    def _(i):
        out[i] = 0
        out[slots + i] = -1
        out[2 * slots + i] = 0
        out[3 * slots + i] = 0
        out[4 * slots + i] = -1
        out[5 * slots + i] = 0

    @pl.loop(0, nrow + ncol)
    def _(i):
        lens[i] = 0

    @pl.loop(0, counts[0, 0])
    def _(k):
        row = rows[k] % span
        col = cols[k]
        o = row // blk
        at = o * capf + lens[o]
        lens[o] = lens[o] + 1
        dev = col // span
        src = dev * blk + col % blk
        out[at] = k
        out[slots + at] = row % blk
        out[2 * slots + at] = src
        bt = dev * capb + lens[ncol + dev]
        lens[ncol + dev] = lens[ncol + dev] + 1
        out[3 * slots + bt] = k
        out[4 * slots + bt] = col % blk
        out[5 * slots + bt] = row


def add_rows(dst, srcs, begin, count):
    step = 64

    @pl.loop(0, count // step)
    def _(i):
        at = pl.ds(pl.multiple_of(begin + i * step, step), step)
        total = srcs[0][at, :].astype(F32)
        for s in srcs[1:]:
            total = total + s[at, :].astype(F32)
        dst[at, :] = total.astype(dst.dtype)


def weight_block(parts, scale, agg, gp, wp):
    width = agg.shape[1]
    rows = width // (2 * parts)
    total = jnp.sum(gp[...].astype(F32), axis=0, keepdims=True) * scale
    pad = jnp.broadcast_to(total, (PAD, width)).astype(BF)
    step = 128
    for t in range(width // step):
        res = lax.dot_general(
            agg[:, t * step : (t + 1) * step],
            gp[...],
            (((0,), (0,)), ((), ())),
            preferred_element_type=F32,
        )
        res = (res * scale).astype(BF)
        for u in range(step // rows):
            p = (t * step) // rows + u
            wp[p // parts, p % parts, :rows, :] = res[u * rows : (u + 1) * rows]
            wp[p // parts, p % parts, rows:, :] = pad


def mega_kernel(
    names, n, nrow, nb, scale, wf, wb, lists, feats, tiles_in, w_in, bias, cot_in, out, fg, wg, bg,
    *scratch
):
    v = types.SimpleNamespace(**dict(zip(names, scratch)))
    r, q = lax.axis_index("row"), lax.axis_index("col")
    k, c = r // 2, r % 2
    chips = nrow // 2
    last = n - 1
    right, left = (r, jnp.minimum(q + 1, last)), (r, jnp.maximum(q - 1, 0))
    partner = (k * 2 + 1 - c, q)
    relay = chips == 4
    near = [d for d in range(1, chips) if not (relay and d == 3)]
    hb = nb // 2
    slots, size = v.tiles.shape[0], v.tiles.shape[1]
    rows = nb * size
    capf, capb = slots // n, slots // nrow
    kparts = capf // capb
    nch, ng = len(wf), len(wb)
    w, cot = v.w, v.cot
    npa = v.pa.shape[0] // n
    npc = npa // (nch - 1)
    arows = rows // npc
    npb = v.pb.shape[0] // n
    piece = rows // npb
    ppb = size // piece
    xg = [getattr(v, "x%d" % j) for j in range(nch)]
    sp, grads, abuf, bbuf, cbuf, fgs = (
        [getattr(v, "%s%d" % (name, g)) for g in range(ng)]
        for name in ("sp", "g", "a", "b", "c", "f")
    )

    def dev(d):
        return (flip(k, d) * 2 + c, q)

    def deep(dz):
        return (r, (q + dz) % n)


    def take(j):
        return pltpu.make_async_copy(
            feats.at[:, :, pl.ds(sum(wf[:j]), wf[j])], xg[j].at[pl.ds(r * nb, nb)], v.s_take.at[j]
        )

    def slot(j, d, core, h):
        return xg[j].at[pl.ds((flip(k, d) * 2 + core) * nb + h * hb, hb)]

    def same(j, d, h, to, at):
        ref = slot(j, d, c, h)
        return remote(ref, ref, v.s_same.at[j], v.r_same.at[j, at, h], dev(to))

    def own(j, d, h):
        return same(j, 0, h, d, d)

    def pass_on(j, h):
        via, to = (1, 2) if h == 0 else (2, 1)
        return same(j, via, h, to, 3)

    def inc(j, d, h):
        return same(j, d, h, d, d)

    def fwd(j, d, h):
        ref = slot(j, d, c, h)
        return remote(ref, ref, v.s_part.at[j], v.r_part.at[j], partner)

    def gather_start(j, parts=(0, 1)):
        if parts[0] == 0:
            take(j).wait()
        for i in parts:
            for d in near:
                own(j, d, (i + (d == 2)) % 2).start()
            fwd(j, 0, i).start()

    def gather_mid(j):
        for i in range(2):
            for d in near:
                h = (i + (d == 2)) % 2
                inc(j, d, h).wait_recv()
                if relay and i == 0:
                    pass_on(j, h).start()
                fwd(j, d, h).start()

    def whole(j, count):
        ref = xg[j].at[pl.ds(0, count * nb)]
        return remote(ref, ref, v.s_part.at[j], v.r_part.at[j], partner)

    def gather_end(j):
        if relay:
            for h in range(2):
                inc(j, 3, h).wait_recv()
                fwd(j, 3, h).start()
        whole(j, chips).wait_recv()

    def gather_sent(j):
        ref = xg[j].at[pl.ds(0, (chips - 1) * nb)]
        remote(ref, ref, v.s_same.at[j], v.r_same.at[j, 0, 0], partner).wait_send()
        whole(j, chips).wait_send()


    def build(o, base, cap, back):
        for s in range(cap):
            at = o * cap + s
            mat = v.tiles[lists[base * slots + at]]
            place = lists[(base + 1) * slots + at]
            if back:
                mat = jnp.transpose(mat)
            for b in range(nb):
                val = jnp.where(place == b, mat, jnp.zeros_like(mat))
                if back:
                    v.dense[o, b * size : (b + 1) * size, s * size : (s + 1) * size] = val
                else:
                    u = s % capb
                    v.dense[
                        o * kparts + s // capb, b * size : (b + 1) * size, u * size : (u + 1) * size
                    ] = val

    def forward(j):
        @pl.loop(0, n)
        def _(o):
            total = None
            for e in range(kparts):
                ids = [lists[2 * slots + o * capf + e * capb + s] for s in range(capb)]
                rhs = jnp.concatenate([xg[j][i] for i in ids], axis=0)
                res = jnp.dot(v.dense[o * kparts + e], rhs, preferred_element_type=F32)
                total = res if total is None else total + res
            total = total.astype(BF)
            if j < nch - 1:
                v.pa[pl.ds(o * npa + j * npc, npc)] = total.reshape(npc, arows, wf[j])
            else:
                v.pb[pl.ds(o * npb, npb)] = total.reshape(npb, piece, wf[j])

    def backward(g, o):
        ids = [lists[5 * slots + o * capb + s] for s in range(capb)]
        rhs = jnp.concatenate([sp[g][i] for i in ids], axis=0)
        grads[g][o] = jnp.dot(v.dense[o], rhs, preferred_element_type=F32).astype(BF)


    def chain(part, acc, count, send, recv, to, shift, d, j, first):
        at = (d + shift) * count + j
        src = part.at[d * count + j] if first else acc.at[at]
        return remote(src, acc.at[at], send.at[shift, d], recv.at[d + shift, j], to)

    def group(part, acc, count, send, recv):
        def cp_r(d, j, first=False):
            return chain(part, acc, count, send, recv, right, 1, d, j, first)

        def cp_l(d, j, first=False):
            return chain(part, acc, count, send, recv, left, 0, d, j, first)

        def hop(cp, shift, start, d, j):
            @pl.when(start)
            def _():
                cp(d, j, True).start()

            @pl.when(jnp.logical_not(start))
            def _():
                cp(d, j).wait_recv()
                at = (d + shift) * count + j
                acc[at] = (acc[at].astype(F32) + part[d * count + j].astype(F32)).astype(BF)
                cp(d, j).start()

        def live(j):
            return jnp.logical_and(j >= 0, j < count)

        def reduce_step(t):
            jr, jl = t - HOP * q, t - HOP * (last - q)

            @pl.when(live(jr))
            def _():
                @pl.loop(0, last - q)
                def _(i):
                    hop(cp_r, 1, q == 0, last - i, jr)

            @pl.when(live(jl))
            def _():
                @pl.loop(0, q)
                def _(i):
                    hop(cp_l, 0, q == last, i, jl)

        def total(j, buf):
            buf[...] = part[q * count + j].astype(F32)

            @pl.when(q > 0)
            def _():
                cp_r(q, j).wait_recv()
                buf[...] += acc[(q + 1) * count + j].astype(F32)

            @pl.when(q < last)
            def _():
                cp_l(q, j).wait_recv()
                buf[...] += acc[q * count + j].astype(F32)

        def sent():
            for d in range(n):
                ref = part.at[pl.ds(d * count, count)]

                @pl.when(q < d)
                def _():
                    remote(ref, ref, send.at[1, d], recv.at[0, 0], right).wait_send()

                @pl.when(q > d)
                def _():
                    remote(ref, ref, send.at[0, d], recv.at[0, 0], left).wait_send()

        return types.SimpleNamespace(live=live, reduce_step=reduce_step, total=total, sent=sent)

    ga = group(v.pa, v.acca, npa, v.s_ra, v.r_ra)
    gb = group(v.pb, v.accb, npb, v.s_rb, v.r_rb)


    def part_of(d, j):
        at = d * npb + j
        return at // ppb, pl.ds(pl.multiple_of((at % ppb) * piece, piece), piece)

    def cp_g(side, to, d, j):
        b, at = part_of(d, j)
        ref = sp[0].at[b, at]
        return remote(ref, ref, v.s_g.at[side, d], v.r_g.at[d, j], to)

    cp_gr = functools.partial(cp_g, 1, right)
    cp_gl = functools.partial(cp_g, 0, left)

    def cp_h(g, side, to, d, h):
        ref = sp[g].at[pl.ds(d * nb + h * hb, hb)]
        return remote(ref, ref, v.s_h.at[g - 1, side, d], v.r_h.at[g - 1, d, h], to)

    def cp_hr(g):
        return functools.partial(cp_h, g, 1, right)

    def cp_hl(g):
        return functools.partial(cp_h, g, 0, left)

    def send_both(cr, cl, d, j):
        @pl.when(q < last)
        def _():
            cr(d, j).start()

        @pl.when(q > 0)
        def _():
            cl(d, j).start()

    def relay_on(cr, cl, ok, j, o):
        @pl.when(jnp.logical_and(ok, q >= o))
        def _():
            cr(q - o, j).wait_recv()

            @pl.when(q < last)
            def _():
                cr(q - o, j).start()

        @pl.when(jnp.logical_and(ok, q + o <= last))
        def _():
            cl(q + o, j).wait_recv()

            @pl.when(q > 0)
            def _():
                cl(q + o, j).start()

    def own_rest(g):
        for h in range(2):
            send_both(cp_hr(g), cp_hl(g), q, h)

    def relay_rest(g, o):
        for i in range(o, n if o == 3 else min(o + 1, n)):
            for h in range(2):
                relay_on(cp_hr(g), cp_hl(g), True, h, i)

    def sent_on(g):
        send = v.s_g if g == 0 else v.s_h.at[g - 1]
        recv = v.r_g.at[0, 0]
        for d in range(n):
            ref = sp[g].at[pl.ds(d * nb, nb)]

            @pl.when(jnp.logical_and(q >= d, q < last))
            def _():
                remote(ref, ref, send.at[1, d], recv, right).wait_send()

            @pl.when(jnp.logical_and(q <= d, q > 0))
            def _():
                remote(ref, ref, send.at[0, d], recv, left).wait_send()

    def finish_a(j):
        ga.total(j, v.fa)
        e, i = j // npc, j % npc
        v.agg[i * arows : (i + 1) * arows, e * wf[0] : (e + 1) * wf[0]] = v.fa[...].astype(BF)

    def finish(j):
        gb.total(j, v.fb)
        at = pl.ds(pl.multiple_of(j * piece, piece), piece)
        v.agg[at, sum(wf[:-1]) :] = v.fb[...].astype(BF)
        pre = jnp.dot(v.agg[at, :], w[...], preferred_element_type=F32) + bias[...]
        sig = jax.nn.sigmoid(pre)
        v.out[at, :] = (pre * sig).astype(BF)
        grad = (cot[at, :].astype(F32) * sig * (1.0 + pre * (1.0 - sig))).astype(BF)
        v.gp[at, :] = grad
        res = lax.dot_general(
            grad, w[...], (((1,), (1,)), ((), ())), preferred_element_type=F32
        ).astype(BF)
        b, sub = part_of(q, j)
        for g in range(ng):
            sp[g][b, sub, :] = res[:, sum(wb[:g]) : sum(wb[: g + 1])]
        send_both(cp_gr, cp_gl, q, j)


    cp_w1 = remote(v.wp.at[1 - c], v.w1, v.s_w.at[0], v.r_w.at[0], partner)
    w4 = v.w4

    def cp_w2(d):
        return remote(v.w1.at[flip(k, d)], v.w2.at[d - 1], v.s_w.at[1], v.r_w.at[1], dev(d))

    def cp_w3(dz):
        return remote(v.ws, v.w3.at[dz - 1], v.s_w.at[2], v.r_w.at[2], deep(dz))

    def cp_w4(d):
        return remote(w4.at[c, k], w4.at[c, k], v.s_w.at[3], v.r_w.at[3], dev(d))

    cp_w5 = remote(w4.at[c], w4.at[c], v.s_w.at[4], v.r_w.at[4], partner)

    def all_w(ref, i):
        return remote(ref, ref, v.s_w.at[i], v.r_w.at[i], partner)

    all_w2 = all_w(v.w2, 1)
    all_w3 = all_w(v.w3, 2)
    all_w4 = all_w(w4.at[0, pl.ds(0, chips - 1)], 3)

    def weight_0():
        weight_block(chips, scale, v.agg, v.gp, v.wp)
        cp_w1.start()

    def weight_1():
        cp_w1.wait_recv()
        for z in range(chips):
            v.w1[z] = (v.w1[z].astype(F32) + v.wp[c, z].astype(F32)).astype(BF)
        for d in range(chips - 1, 0, -1):
            cp_w2(d).start()

    def weight_2():
        all_w2.wait_recv()
        total = v.w1[k].astype(F32)
        for d in range(1, chips):
            total = total + v.w2[d - 1].astype(F32)
        v.ws[...] = total.astype(BF)
        for dz in range(1, n):
            cp_w3(dz).start()

    def weight_3():
        all_w3.wait_recv()
        total = None
        for i in range(n):
            other = v.w3[jnp.maximum((q - i + n) % n - 1, 0)].astype(F32)
            term = jnp.where(q == i, v.ws[...].astype(F32), other)
            total = term if total is None else total + term
        w4[c, k] = total.astype(BF)
        for d in range(chips - 1, 0, -1):
            cp_w4(d).start()

    def weight_4():
        all_w4.wait_recv()
        cp_w5.start()

    store_w = pltpu.make_async_copy(w4, wg, v.s_load.at[1])

    def weight_5():
        remote(
            w4.at[1 - c], w4.at[1 - c], v.s_w.at[4], v.r_w.at[4], partner
        ).wait_recv()
        bg[...] = w4[0, 0, w4.shape[2] - PAD :, :].astype(F32)[:1]
        store_w.start()

    def weight_sent():
        cp_w1.wait_send()
        for a in (all_w2, all_w3, all_w4, cp_w5):
            a.wait_send()
        store_w.wait()


    half = rows // 2

    def mine(g, d):
        return grads[g].at[flip(k, d) * 2 + c]

    def cp_a(g, d):
        return remote(
            grads[g].at[flip(k, d) * 2 + 1 - c],
            abuf[g].at[d],
            v.s_a.at[g],
            v.r_a.at[g, d],
            partner,
        )

    def cp_b(g, d, h):
        at = pl.ds(h * half, half)
        i = near.index(d)
        return remote(abuf[g].at[d, at], bbuf[g].at[i, at], v.s_b.at[g], v.r_b.at[g], dev(d))

    def all_b(g):
        return remote(bbuf[g], bbuf[g], v.s_b.at[g], v.r_b.at[g], partner)

    def cp_c(g, h):
        return remote(
            abuf[g].at[3, pl.ds(h * half, half)],
            cbuf[g].at[h],
            v.s_c.at[g],
            v.r_c.at[g, h],
            dev(h + 1),
        )

    def join(g, d):
        cp_a(g, d).wait_recv()
        add_rows(abuf[g].at[d], [abuf[g].at[d], mine(g, d)], 0, rows)

    def pass_first(g, d):
        join(g, d)
        if not relay:
            for h in range(2):
                cp_b(g, d, h).start()
        elif d == 3:
            for h in range(2):
                cp_c(g, h).start()
        else:
            cp_b(g, d, d - 1).start()

    def products(g, part):
        for i in range(part * chips // PARTS, (part + 1) * chips // PARTS):
            d = chips - 1 - i
            at = flip(k, d) * 2
            backward(g, at + 1 - c)
            cp_a(g, d).start()
            backward(g, at + c)
            if i > 0:
                pass_first(g, d + 1)

    def rows_2(g):
        if relay:
            cp_c(g, 0).wait_recv()
            add_rows(abuf[g].at[2], [abuf[g].at[2], cbuf[g].at[0]], 0, half)
            cp_b(g, 2, 0).start()
            cp_c(g, 1).wait_recv()
            at = pl.ds(half, half)
            add_rows(abuf[g].at[1, at], [abuf[g].at[1, at], cbuf[g].at[1]], 0, half)
            cp_b(g, 1, 1).start()
        join(g, 0)

    def store(g):
        return pltpu.make_async_copy(
            fgs[g], fg.at[:, pl.ds(sum(wb[:g]), wb[g])], v.s_store.at[g]
        )

    def rows_3(g):
        all_b(g).wait_recv()
        add_rows(fgs[g], [abuf[g].at[0]] + [bbuf[g].at[i] for i in range(len(near))], 0, rows)
        store(g).start()

    def rows_sent(g):
        remote(
            grads[g].at[pl.ds(0, chips)], abuf[g], v.s_a.at[g], v.r_a.at[g, 0], partner
        ).wait_send()
        all_b(g).wait_send()
        if relay:
            remote(cbuf[g], cbuf[g], v.s_c.at[g], v.r_c.at[g, 0], partner).wait_send()
        store(g).wait()


    barrier = pltpu.get_barrier_semaphore()
    peers = [partner] + [dev(d) for d in range(1, chips)] + [deep(dz) for dz in range(1, n)]
    for peer in peers:
        pl.semaphore_signal(barrier, inc=1, device_id=peer, device_id_type=MESH)
    loads = [
        pltpu.make_async_copy(a, b, v.s_load.at[i])
        for i, (a, b) in enumerate([(tiles_in, v.tiles), (w_in, w), (cot_in, cot)])
    ]
    store_out = pltpu.make_async_copy(v.out, out, v.s_load.at[0])
    for j in range(nch):
        take(j).start()
    for load in loads:
        load.start()
    pl.semaphore_wait(barrier, len(peers))

    gather_start(0)
    for load in loads:
        load.wait()

    @pl.loop(0, n)
    def _(o):
        build(o, 0, capf, False)

    gather_mid(0)
    gather_start(1)
    gather_start(2, (0,))
    gather_end(0)
    forward(0)
    ga.reduce_step(0)
    gather_mid(1)
    gather_start(2, (1,))
    ga.reduce_step(1)
    gather_end(1)
    forward(1)
    ga.reduce_step(2)
    gather_mid(2)
    ga.reduce_step(3)
    gather_end(2)
    forward(2)

    begin = 4
    wait = HOP * last
    done = npa + npb + wait - 1

    @pl.loop(begin, npa + npb + wait + RING * last)
    def _(t):
        ga.reduce_step(t)
        gb.reduce_step(t - npa)

        for e in range(npa):
            @pl.when(t == max(begin, wait + e))
            def _():
                finish_a(e)

        j = t - npa - wait

        @pl.when(gb.live(j))
        def _():
            finish(j)

        for o in range(1, n):
            p = j - RING * o
            relay_on(cp_gr, cp_gl, gb.live(p), p, o)

        o = t - begin

        @pl.when(jnp.logical_and(o >= 0, o < nrow))
        def _():
            build(o, 3, capb, True)

        @pl.when(t == done)
        def _():
            own_rest(1)
            weight_0()
            weight_1()
            store_out.start()

    relay_rest(1, 1)
    products(0, 0)
    own_rest(2)
    products(0, 1)
    products(0, 2)
    products(0, 3)
    relay_rest(1, 2)
    relay_rest(1, 3)
    weight_2()
    rows_2(0)
    relay_rest(2, 1)
    products(1, 0)
    products(1, 1)
    products(1, 2)
    products(1, 3)
    rows_3(0)
    rows_2(1)
    relay_rest(2, 2)
    weight_3()
    relay_rest(2, 3)
    products(2, 0)
    products(2, 1)
    products(2, 2)
    products(2, 3)
    rows_3(1)
    for j in range(nch):
        gather_sent(j)
    ga.sent()
    gb.sent()
    rows_2(2)
    weight_4()
    weight_5()
    for g in range(ng):
        sent_on(g)
    for g in range(ng - 1):
        rows_sent(g)
    rows_3(2)

    rows_sent(ng - 1)
    weight_sent()
    store_out.wait()


def tail_kernel(out_in, fg_in, parts, bg_in, out, fg, wg, bg):
    out[...] = out_in[...]
    fg[...] = fg_in[...]
    count = parts.shape[1]
    rows = wg.shape[0] // (2 * count)
    for a in range(2):
        for b in range(count):
            at = (a * count + b) * rows
            wg[at : at + rows, :] = parts[a, b, :rows, :].astype(F32)
    bg[...] = bg_in[...]


VM = pl.BlockSpec(memory_space=pltpu.VMEM)
SM = pl.BlockSpec(memory_space=pltpu.SMEM)
ANY = pl.BlockSpec(memory_space=pl.ANY)


def dma(*shape):
    return pltpu.SemaphoreType.DMA(shape)


def on_device(features, weight, bias, cotangent, tile_values, tile_rows, tile_cols, tile_counts):
    nrow = lax.axis_size("row")
    ncol = lax.axis_size("col")
    node_dev, width = features.shape
    slots, size = tile_values.shape[2], tile_values.shape[3]
    nb = node_dev // size
    chips = nrow // 2
    scale = 1.0 / math.sqrt(node_dev * nrow * ncol)
    values = tile_values.reshape(slots, size, size)

    lists = pl.pallas_call(
        functools.partial(list_kernel, nrow, ncol, nb),
        out_shape=jax.ShapeDtypeStruct((LISTS * slots,), jnp.int32),
        in_specs=[SM, SM, SM],
        out_specs=SM,
        scratch_shapes=[pltpu.SMEM((nrow + ncol,), jnp.int32)],
        name="lists",
    )(tile_counts, tile_rows.reshape(slots), tile_cols.reshape(slots))

    wf = (width // 4, width // 4, width - 2 * (width // 4))
    wb = (width // 2, width // 4, width - width // 2 - width // 4)
    nch, ng = len(wf), len(wb)
    npa = 4
    arows = node_dev * (nch - 1) // npa
    piece = size // 2
    npb = node_dev // piece
    pr = width // (2 * chips) + PAD
    capb = slots // nrow

    def vm(*shape, dtype=BF):
        return pltpu.VMEM(shape, dtype)

    scratch = {"x%d" % j: vm(nrow * nb, size, wf[j]) for j in range(nch)}
    scratch.update(
        tiles=vm(slots, size, size),
        dense=vm(nrow, node_dev, capb * size),
        pa=vm(ncol * npa, arows, wf[0]),
        pb=vm(ncol * npb, piece, wf[-1]),
        acca=vm((ncol + 1) * npa, arows, wf[0]),
        accb=vm((ncol + 1) * npb, piece, wf[-1]),
        fa=vm(arows, wf[0], dtype=F32),
        fb=vm(piece, wf[-1], dtype=F32),
        w=vm(width, width),
        cot=vm(node_dev, width),
        agg=vm(node_dev, width),
        gp=vm(node_dev, width),
        wp=vm(2, chips, pr, width),
        w1=vm(chips, pr, width),
        w2=vm(chips - 1, pr, width),
        w3=vm(ncol - 1, pr, width),
        w4=vm(2, chips, pr, width),
        out=vm(node_dev, width),
        ws=vm(pr, width),
        s_take=dma(nch),
        s_load=dma(3),
        s_same=dma(nch),
        r_same=dma(nch, chips, 2),
        s_part=dma(nch),
        r_part=dma(nch),
        s_ra=dma(2, ncol),
        r_ra=dma(ncol + 1, npa),
        s_rb=dma(2, ncol),
        r_rb=dma(ncol + 1, npb),
        s_g=dma(2, ncol),
        r_g=dma(ncol, npb),
        s_h=dma(ng - 1, 2, ncol),
        r_h=dma(ng - 1, ncol, 2),
        s_a=dma(ng),
        r_a=dma(ng, chips),
        s_b=dma(ng),
        r_b=dma(ng),
        s_c=dma(ng),
        r_c=dma(ng, 2),
        s_w=dma(5),
        r_w=dma(5),
        s_store=dma(ng),
    )
    others = chips - 1 - (chips == 4)
    for g in range(ng):
        scratch["sp%d" % g] = vm(ncol * nb, size, wb[g])
        scratch["g%d" % g] = vm(nrow, node_dev, wb[g])
        scratch["a%d" % g] = vm(chips, node_dev, wb[g])
        scratch["b%d" % g] = vm(others, node_dev, wb[g])
        scratch["c%d" % g] = vm(2, node_dev // 2, wb[g])
        scratch["f%d" % g] = vm(node_dev, wb[g])

    out, fg, parts, bg = pl.pallas_call(
        functools.partial(mega_kernel, tuple(scratch), ncol, nrow, nb, scale, wf, wb),
        out_shape=[
            jax.ShapeDtypeStruct((node_dev, width), BF),
            jax.ShapeDtypeStruct((node_dev, width), BF),
            jax.ShapeDtypeStruct((2, chips, pr, width), BF),
            jax.ShapeDtypeStruct((1, width), F32),
        ],
        in_specs=[SM, ANY, ANY, ANY, VM, ANY],
        out_specs=[ANY, ANY, ANY, VM],
        scratch_shapes=list(scratch.values()),
        compiler_params=pltpu.CompilerParams(
            collective_id=0, has_side_effects=True, vmem_limit_bytes=60 << 20
        ),
        name="layer",
    )(
        lists,
        features.reshape(nb, size, width),
        values,
        weight,
        bias.reshape(1, width),
        cotangent,
    )

    out, fg, wg, bg = pl.pallas_call(
        tail_kernel,
        out_shape=[
            jax.ShapeDtypeStruct((node_dev, width), BF),
            jax.ShapeDtypeStruct((node_dev, width), BF),
            jax.ShapeDtypeStruct((width, width), F32),
            jax.ShapeDtypeStruct((1, width), F32),
        ],
        in_specs=[VM] * 4,
        out_specs=[VM] * 4,
        name="tail",
    )(out, fg, parts, bg)
    return (out, fg, wg, bg.reshape(width))


def solution(mesh):
    return jax.shard_map(
        on_device,
        mesh=mesh,
        in_specs=(
            P(("row", "col"), None),
            P(),
            P(),
            P(("row", "col"), None),
            P("row", "col", None, None, None),
            P("row", "col", None),
            P("row", "col", None),
            P("row", "col"),
        ),
        out_specs=(P(("row", "col"), None), P(("row", "col"), None), P(), P()),
        check_vma=False,
    )
```
